128 devices in a mesh: ga: 4 (over x), dev: 32 (over z, y, core).
Axes of the slice: x: 4, y: 4, z: 4, core: 2. Of those that a mesh axis runs over, the one named last changes fastest.
Arguments:
- column_state: float32 [6, 72, 65536], P(None, None, ('ga', 'dev')), may hold values from -6 to 6
- neighbours: int32 [16384, 4], P(('ga', 'dev')), may hold values from 0 to 16383, as said below
- crm_slot: int32 [65536], P(('ga', 'dev')), may hold values from 0 to 65535, as said below
- cloudy: int32 [65536], P(('ga', 'dev')), may hold values 0 or 1
- crm_theta: bfloat16 [58, 32, 65536], P(None, None, ('ga', 'dev')), may hold values from -6 to 6
- crm_water: bfloat16 [58, 32, 65536], P(None, None, ('ga', 'dev')), may hold values from -6 to 6
Outputs:
- new_state: float32 [6, 72, 65536], P(None, None, ('ga', 'dev'))
- new_theta: bfloat16 [58, 32, 65536], P(None, None, ('ga', 'dev'))
- new_water: bfloat16 [58, 32, 65536], P(None, None, ('ga', 'dev'))
The draws below stay inside these ranges and needn't reach their ends.
Inputs may be any that keep to these rules, and one draw needn't show every extreme that they name: Each element's neighbours lie among the elements of the same device, of the device before or of the device after it in the order of ga+dev, wrapping around; each device holds 128 elements in order. crm_slot is a permutation of the slots; slot // 512 is the device that runs the column's cloud model. Every device sends exactly 4 of its columns to every device, and slot % 512 equals the sending device's index times 4 plus the column's rank among those 4.
All inputs are finite; a program needn't handle non-finite values. No bound on the sum of `cloudy` on one device may be relied on, other than what follows from the above.
Results may differ from the reference program's by a relative error of at most 0.001.
Values sent between devices are 32-bit elements; how exact they have to be, the bound alone decides.
A program may use at most 128 MiB of HBM per device.

```python
import jax
import jax.numpy as jnp
from jax import lax

FIELDS = 6
LEV = 72
NZC = 58
NXC = 32
SUB = 2
COL_DEV = 512
ELEM_DEV = 128
COLS = 65536
ELEMS = 16384


def draw_neighbours(key, part):
    devices = ELEMS // ELEM_DEV
    key_step, key_local = jax.random.split(jax.random.fold_in(key, 11))
    moves = jax.random.randint(key_step, (ELEMS, 4), -1, 2)
    within = jax.random.randint(key_local, (ELEMS, 4), 0, ELEM_DEV)
    owner = (jnp.arange(ELEMS, dtype=jnp.int32) // ELEM_DEV)[:, None]
    return ((owner + moves) % devices * ELEM_DEV + within).astype(jnp.int32)


def draw_crm_slot(key, part):
    devices = COLS // COL_DEV
    per_peer = COL_DEV // devices
    scores = jax.random.randint(jax.random.fold_in(key, 23), (devices, COL_DEV), 0, 2 ** 16) * COL_DEV
    scores = scores + jnp.arange(COL_DEV, dtype=jnp.int32)[None, :]
    ranking = jnp.argsort(jnp.argsort(scores, axis=1), axis=1).astype(jnp.int32)
    source = jnp.arange(devices, dtype=jnp.int32)[:, None]
    slots = ranking // per_peer * COL_DEV + source * per_peer + ranking % per_peer
    return slots.reshape(COLS).astype(jnp.int32)


def place_ends(entries, key, low, high):
    index_at = [jax.random.randint(jax.random.fold_in(key, axis), (), 0, length) for axis, length in enumerate(entries.shape)]
    widest = entries.shape.index(max(entries.shape))
    neighbour = index_at[:widest] + [(index_at[widest] + 1) % entries.shape[widest]] + index_at[widest + 1:]
    return entries.at[tuple(index_at)].set(low).at[tuple(neighbour)].set(high)


def block_levels(rng, extent, cuts, low, largest):
    factor_of, own = 1.0, jax.random.fold_in(rng, 6)
    for dim, shards_of in cuts:
        heights = jnp.exp(jax.random.uniform(jax.random.fold_in(own, dim), (shards_of,), jnp.float32, low / len(cuts), largest / len(cuts)))
        factor_of = factor_of * jnp.repeat(heights, extent[dim] // shards_of).reshape([-1 if axis == dim else 1 for axis in range(len(extent))])
    return factor_of


def gaussian(rng, dims, scale, bound, cuts=(), kind=jnp.bfloat16):
    values = scale * jax.random.normal(rng, dims, jnp.float32)
    if cuts:
        values = values * block_levels(rng, dims, cuts, -0.22, 0.18)
    return jnp.clip(values, -bound, bound).astype(kind)


def setup_inputs(seed: int = 0) -> dict:
    splits = jax.random.split(jax.random.key(seed), 7)
    return {
        "column_state": gaussian(splits[0], (FIELDS, LEV, COLS), 1.0, 6.0, ((2, 128),), jnp.float32),
        "neighbours": draw_neighbours(jax.random.fold_in(splits[6], 71), 0),
        "crm_slot": draw_crm_slot(jax.random.fold_in(splits[6], 71), 0),
        "cloudy": place_ends((jax.random.randint(splits[3], (COLS,), 0, 2) < 1).astype(jnp.int32), jax.random.fold_in(splits[3], 1), 0, 1),
        "crm_theta": gaussian(splits[4], (NZC, NXC, COLS), 1.0, 6.0, ((2, 128),)),
        "crm_water": gaussian(splits[5], (NZC, NXC, COLS), 1.0, 6.0, ((2, 128),)),
    }


DIFFUSION = 0.15
X_DIFFUSION = 0.2
RELAX_RATE = 0.2
LATENT_HEAT = 0.8
STEP_WEIGHT = 0.5


def advect(profile, advection):
    east_side = jnp.roll(profile, -1, axis=1)
    west_side = jnp.roll(profile, 1, axis=1)
    return profile - 0.5 * advection * (east_side - west_side) + X_DIFFUSION * (east_side - 2.0 * profile + west_side)


def vertical_mix(profile, mixing):
    upper_cell = jnp.concatenate([profile[1:], profile[-1:]], axis=0)
    lower_cell = jnp.concatenate([profile[:1], profile[:-1]], axis=0)
    return profile + mixing * (upper_cell - 2.0 * profile + lower_cell)


def crm_block(large_scale, crm_theta, crm_water, cloudy):
    crm_levels = crm_theta.shape[0]
    low_levels = large_scale[:, :crm_levels]
    advection = (0.3 * jnp.tanh(low_levels[0]))[:, None, :]
    mixing = (0.1 + 0.15 * jax.nn.sigmoid(low_levels[1]))[:, None, :]
    target_heat = low_levels[2]
    moisture = low_levels[3]
    target_water = moisture + low_levels[4] + low_levels[5]
    flagged = cloudy.astype(jnp.float32)[None, None, :]
    theta_now = crm_theta.astype(jnp.float32)
    water_now = crm_water.astype(jnp.float32)
    condensed = jnp.zeros_like(theta_now)
    for substep in range(SUB):
        theta_now = vertical_mix(advect(theta_now, advection), mixing)
        water_now = vertical_mix(advect(water_now, advection), mixing)
        theta_now = theta_now + RELAX_RATE * (target_heat - jnp.mean(theta_now, axis=1))[:, None, :]
        water_now = water_now + RELAX_RATE * (target_water - jnp.mean(water_now, axis=1))[:, None, :]
        excess = flagged * 0.5 * jnp.maximum(water_now - 0.5 * theta_now - 0.5, 0.0)
        water_now = water_now - excess
        theta_now = theta_now + LATENT_HEAT * excess
        condensed = condensed + excess
    tendency = jnp.stack([jnp.mean(theta_now, axis=1) - target_heat,
                          jnp.mean(water_now, axis=1) - moisture,
                          jnp.mean(condensed, axis=1) - low_levels[4]])
    return tendency, theta_now.astype(jnp.bfloat16), water_now.astype(jnp.bfloat16)


def dynamics(column_state, neighbours):
    fields, levels, columns = column_state.shape
    element_mean = jnp.mean(column_state.reshape(fields, levels, columns // 4, 4), axis=-1)
    nearby = jnp.sum(jnp.take(element_mean, neighbours, axis=2), axis=-1)
    laplace = nearby - 4.0 * element_mean
    return column_state + DIFFUSION * jnp.repeat(laplace, 4, axis=2)


def reference(column_state, neighbours, crm_slot, cloudy, crm_theta, crm_water):
    dynamics_state = dynamics(column_state, neighbours)
    columns = column_state.shape[2]
    inverse = jnp.zeros((columns,), jnp.int32).at[crm_slot].set(jnp.arange(columns, dtype=jnp.int32))
    slot_state = jnp.take(dynamics_state, inverse, axis=2)
    blocks = columns // COL_DEV

    def one_block(block_index):
        first_slot = (block_index * COL_DEV).astype(jnp.int32)
        return crm_block(lax.dynamic_slice_in_dim(slot_state, first_slot, COL_DEV, 2),
                         lax.dynamic_slice_in_dim(crm_theta, first_slot, COL_DEV, 2),
                         lax.dynamic_slice_in_dim(crm_water, first_slot, COL_DEV, 2),
                         lax.dynamic_slice_in_dim(cloudy, first_slot, COL_DEV, 0))

    tendency, theta_blocks, water_blocks = lax.map(one_block, jnp.arange(blocks, dtype=jnp.int32))
    tendency = jnp.transpose(tendency, (1, 2, 0, 3)).reshape(3, NZC, columns)
    new_theta = jnp.transpose(theta_blocks, (1, 2, 0, 3)).reshape(NZC, NXC, columns)
    new_water = jnp.transpose(water_blocks, (1, 2, 0, 3)).reshape(NZC, NXC, columns)
    column_tendency = jnp.take(tendency, crm_slot, axis=2)
    new_state = dynamics_state.at[2:5, :NZC].add(STEP_WEIGHT * column_tendency)
    return new_state, new_theta, new_water
```

```python
import functools

import jax
import jax.numpy as jnp
from jax import lax
from jax.experimental import pallas as pl
from jax.experimental.pallas import tpu as pltpu
from jax.sharding import PartitionSpec as P

SUB = 2
DIFFUSION = 0.15
X_DIFFUSION = 0.2
RELAX_RATE = 0.2
LATENT_HEAT = 0.8
STEP_WEIGHT = 0.5
LANES = 128


def mixed(rows, m, keep, levels):
    up = pltpu.roll(rows, rows.shape[0] - 1, 0)
    down = pltpu.roll(rows, 1, 0)
    z = lax.broadcasted_iota(jnp.int32, rows.shape, 0)
    up = jnp.where(z == levels - 1, rows, up)
    down = jnp.where(z == 0, rows, down)
    return keep * rows + m * (up + down)


def crm_kernel(levels, cells, feat_ref, cloudy_ref, theta_ref, water_ref,
               theta_out, water_out, means_out, th, wa, coef, esum):
    zp = feat_ref.shape[1] // 4
    groups = cells // 8
    fields = jnp.transpose(feat_ref[...], (1, 0))
    u, v, heat, wet = (fields[i * zp:(i + 1) * zp] for i in range(4))
    keep_x = 1.0 - 2.0 * X_DIFFUSION
    a = 0.15 * jnp.tanh(u)
    m = 0.1 + 0.15 * jax.nn.sigmoid(v)
    keep = 1.0 - 2.0 * m
    coef[0] = (X_DIFFUSION - a) / keep_x
    coef[1] = (X_DIFFUSION + a) / keep_x
    coef[2] = keep_x * m
    coef[3] = keep_x * keep
    flag = 0.5 * cloudy_ref[0:1].astype(jnp.float32)
    flag8 = jnp.broadcast_to(flag, (8, LANES))

    def widen(z, _):
        for src, dst, slot in ((theta_ref, th, 0), (water_ref, wa, 1)):
            g = src[z].astype(jnp.float32)
            dst[pl.ds(z * cells, cells), :] = g
            s = g[0:8]
            for k in range(1, groups):
                s = s + g[8 * k:8 * k + 8]
            esum[slot, pl.ds(z, 1), :] = jnp.sum(s, axis=0, keepdims=True)
        return 0
    lax.fori_loop(0, levels, widen, 0, unroll=2)

    inv = 1.0 / cells
    mean_t = esum[0] * inv
    mean_w = esum[1] * inv
    condensed = None

    def load_first(ref, z):
        return [ref[pl.ds(z * cells + k, 8, stride=groups), :] for k in range(groups)]

    def load_next(ref, z):
        return [ref[pl.ds(z * cells + 8 * k, 8), :] for k in range(groups)]

    def row(i, z):
        return jnp.broadcast_to(coef[i, pl.ds(z, 1), :], (8, LANES))

    for step in range(SUB):
        last = step == SUB - 1
        mean_t = mixed(mean_t, m, keep, levels)
        mean_w = mixed(mean_w, m, keep, levels)
        relax_t = RELAX_RATE * (heat - mean_t)
        relax_w = RELAX_RATE * (wet - mean_w)
        coef[4] = relax_t
        coef[5] = relax_w
        coef[6] = relax_w - 0.5 * relax_t - 0.5
        load = load_first if step == 0 else load_next

        def advected(z):
            east_c, west_c = row(0, z), row(1, z)
            out = []
            for ref in (th, wa):
                g = load(ref, z)
                east = g[1:] + [pltpu.roll(g[0], 7, 0)]
                west = [pltpu.roll(g[-1], 1, 0)] + g[:-1]
                out.append([g[k] + (east_c * east[k] + west_c * west[k]) for k in range(groups)])
            return out

        def body(z, carry):
            below, here = carry
            above = advected(jnp.minimum(z + 1, levels - 1))
            mz, kz = row(2, z), row(3, z)
            rt, rw, c = row(4, z), row(5, z), row(6, z)
            total = None
            for k in range(groups):
                t = kz * here[0][k] + mz * (above[0][k] + below[0][k])
                w = kz * here[1][k] + mz * (above[1][k] + below[1][k])
                e = flag8 * jnp.maximum((w - 0.5 * t) + c, 0.0)
                t = (t + rt) + LATENT_HEAT * e
                w = (w + rw) - e
                total = e if total is None else total + e
                if last:
                    th[pl.ds(z * cells + k, 8, stride=groups), :] = t
                    wa[pl.ds(z * cells + k, 8, stride=groups), :] = w
                else:
                    th[pl.ds(z * cells + 8 * k, 8), :] = t
                    wa[pl.ds(z * cells + 8 * k, 8), :] = w
            esum[step, pl.ds(z, 1), :] = jnp.sum(total, axis=0, keepdims=True)
            return here, above

        first = advected(0)
        lax.fori_loop(0, levels, body, (first, first), unroll=2)
        excess = esum[step] * inv
        mean_t = mean_t + relax_t + LATENT_HEAT * excess
        mean_w = mean_w + relax_w - excess
        condensed = excess if condensed is None else condensed + excess

    def narrow(z, _):
        theta_out[z] = th[pl.ds(z * cells, cells), :].astype(theta_out.dtype)
        water_out[z] = wa[pl.ds(z * cells, cells), :].astype(water_out.dtype)
        return 0
    lax.fori_loop(0, levels, narrow, 0, unroll=2)
    means_out[...] = jnp.transpose(jnp.concatenate([mean_t, mean_w, condensed, condensed], axis=0), (1, 0))


def crm(feat, cloudy, theta, water):
    levels, cells, slots = theta.shape
    zp = feat.shape[1] // 4
    blk = pl.BlockSpec((levels, cells, LANES), lambda i: (0, 0, i))
    return pl.pallas_call(
        functools.partial(crm_kernel, levels, cells),
        grid=(slots // LANES,),
        out_shape=(jax.ShapeDtypeStruct(theta.shape, theta.dtype),
                   jax.ShapeDtypeStruct(water.shape, water.dtype),
                   jax.ShapeDtypeStruct((slots, 4 * zp), jnp.float32)),
        in_specs=[pl.BlockSpec((LANES, 4 * zp), lambda i: (i, 0)),
                  pl.BlockSpec((1, LANES), lambda i: (0, i)), blk, blk],
        out_specs=(blk, blk, pl.BlockSpec((LANES, 4 * zp), lambda i: (i, 0))),
        scratch_shapes=[pltpu.VMEM((levels * cells, LANES), jnp.float32),
                        pltpu.VMEM((levels * cells, LANES), jnp.float32),
                        pltpu.VMEM((7, zp, LANES), jnp.float32),
                        pltpu.VMEM((2, zp, LANES), jnp.float32)],
        name="crm",
    )(feat, cloudy.reshape(1, slots), theta, water)


def dot(a, b, dims=(((1,), (0,)), ((), ()))):
    return lax.dot_general(a, b, dims, precision=lax.Precision.HIGHEST, preferred_element_type=jnp.float32)


def on_device(column_state, neighbours, crm_slot, cloudy, crm_theta, crm_water):
    fields, levels, columns = column_state.shape
    elements = columns // 4
    devices = lax.axis_size(("ga", "dev"))
    crm_levels = crm_theta.shape[0]
    zp = 64
    state = column_state.reshape(fields * levels, columns)
    member = (jnp.arange(columns)[:, None] // 4 == jnp.arange(elements)[None, :]).astype(jnp.float32)
    mean = dot(state, 0.25 * member)
    forward = [(i, (i + 1) % devices) for i in range(devices)]
    backward = [(b, a) for a, b in forward]
    low = lax.ppermute(mean, ("ga", "dev"), forward)
    high = lax.ppermute(mean, ("ga", "dev"), backward)
    padded = jnp.concatenate([low, mean, high], axis=1)
    offset = lax.axis_index(("ga", "dev")) * elements
    relative = (neighbours - offset + elements) % (elements * devices)
    count = jnp.sum((relative.T[None] == jnp.arange(3 * elements)[:, None, None]).astype(jnp.float32), axis=1)
    laplace = dot(padded, count) - 4.0 * mean
    dynamics = state + DIFFUSION * dot(laplace, member, (((1,), (1,)), ((), ())))
    per_peer = columns // devices
    dest_row = crm_slot // columns * per_peer + crm_slot % per_peer
    place = (dest_row[None, :] == jnp.arange(columns)[:, None]).astype(jnp.float32)
    grid = dynamics.reshape(fields, levels, columns)
    wet = grid[3] + grid[4] + grid[5]
    sent = jnp.concatenate([grid[:3], wet[None]])[:, :crm_levels]
    sent = jnp.pad(sent, ((0, 0), (0, zp - crm_levels), (0, 0))).reshape(4 * zp, columns)
    outgoing = dot(place, sent, (((1,), (1,)), ((), ())))
    arrived = lax.all_to_all(outgoing.reshape(devices, per_peer, 4 * zp), ("ga", "dev"), 0, 0, tiled=True)
    new_theta, new_water, means = crm(arrived.reshape(columns, 4 * zp), cloudy, crm_theta, crm_water)
    back = lax.all_to_all(means[:, :3 * zp].reshape(devices, per_peer, 3 * zp), ("ga", "dev"), 0, 0, tiled=True)
    after = dot(back.reshape(columns, 3 * zp), place, (((0,), (0,)), ((), ()))).reshape(3, zp, columns)[:, :crm_levels]
    low_part = grid[2:5, :crm_levels]
    updated = low_part + STEP_WEIGHT * (after - low_part)
    changed = jnp.concatenate([updated, grid[2:5, crm_levels:]], axis=1)
    new_state = jnp.concatenate([grid[:2], changed, grid[5:]], axis=0)
    return (new_state, new_theta, new_water)


def solution(mesh):
    return jax.shard_map(
        on_device,
        mesh=mesh,
        in_specs=(
            P(None, None, ("ga", "dev")),
            P(("ga", "dev"), None),
            P(("ga", "dev")),
            P(("ga", "dev")),
            P(None, None, ("ga", "dev")),
            P(None, None, ("ga", "dev")),
        ),
        out_specs=(
            P(None, None, ("ga", "dev")),
            P(None, None, ("ga", "dev")),
            P(None, None, ("ga", "dev")),
        ),
        check_vma=False,
    )
```

```python
import functools

import jax
import jax.numpy as jnp
from jax import lax
from jax.experimental import pallas as pl
from jax.experimental.pallas import tpu as pltpu
from jax.sharding import PartitionSpec as P

SUB = 2
DIFFUSION = 0.15
X_DIFFUSION = 0.2
RELAX_RATE = 0.2
LATENT_HEAT = 0.8
STEP_WEIGHT = 0.5
LANES = 128
ROWS = 8
MESH = pl.DeviceIdType.MESH
F32, BF16 = jnp.float32, jnp.bfloat16


def pieces(x):
    high = x.astype(BF16)
    rest = x - high.astype(F32)
    middle = rest.astype(BF16)
    return high, middle, (rest - middle.astype(F32)).astype(BF16)


def dot(a, b, left=1, right=0):
    dims = (((left,), (right,)), ((), ()))
    one = functools.partial(lax.dot_general, dimension_numbers=dims, preferred_element_type=F32)
    if a.dtype == BF16:
        parts = [one(a, p) for p in pieces(b)]
    else:
        parts = [one(p, b) for p in pieces(a)]
    return (parts[2] + parts[1]) + parts[0]


def iota(shape, dim):
    return lax.broadcasted_iota(jnp.int32, shape, dim)


def ones_where(mask, value=1.0):
    return jnp.where(mask, value, 0.0).astype(BF16)


def mixed(rows, m, keep, levels):
    up = pltpu.roll(rows, rows.shape[0] - 1, 0)
    down = pltpu.roll(rows, 1, 0)
    z = iota(rows.shape, 0)
    up = jnp.where(z == levels - 1, rows, up)
    down = jnp.where(z == 0, rows, down)
    return keep * rows + m * (up + down)


def step_kernel(sizes, state_hbm, nb_ref, slot_ref, cloudy_ref, theta_hbm, water_hbm,
                state_out, theta_out, water_out,
                state, mean, low, high, place, theta_in, water_in, th, wa, coef, esum, base,
                fwd_out, fwd_in, ret_out, ret_in,
                load_sem, halo_send, halo_recv, fwd_send, fwd_recv, ret_send, ret_recv):
    planes, per_plane, levels, cells = sizes
    devices = planes * per_plane
    fields, lev, columns = state.shape
    elements = columns // 4
    peer_rows = columns // devices
    zp = coef.shape[1]
    groups = cells // ROWS
    ga, dev = lax.axis_index("ga"), lax.axis_index("dev")
    me = ga * per_plane + dev

    load_state = pltpu.make_async_copy(state_hbm, state, load_sem.at[0])
    load_state.start()
    loads = []
    for b in range(planes):
        for j, (src, dst) in enumerate(((theta_hbm, theta_in), (water_hbm, water_in))):
            loads.append(pltpu.make_async_copy(
                src.at[:, :, pl.ds(b * LANES, LANES)], dst.at[b], load_sem.at[1 + 2 * b + j]))
            loads[-1].start()

    barrier = pltpu.get_barrier_semaphore()

    def greet(k, _):
        p = lax.rem(me + k, devices)
        pl.semaphore_signal(barrier, inc=1, device_id=(p // per_plane, lax.rem(p, per_plane)), device_id_type=MESH)
        return 0
    lax.fori_loop(1, devices, greet, 0)

    load_state.wait()
    flat = state[...].reshape(fields * lev, columns)
    gather = ones_where(iota((columns, elements), 0) // 4 == iota((columns, elements), 1), 0.25)
    mean[...] = dot(flat, gather)
    pl.semaphore_wait(barrier, devices - 1)

    halo = []
    for j, (shift, dst) in enumerate(((1, low), (devices - 1, high))):
        p = lax.rem(me + shift, devices)
        halo.append(pltpu.make_async_remote_copy(
            mean, dst, halo_send.at[j], halo_recv.at[j],
            device_id=(p // per_plane, lax.rem(p, per_plane)), device_id_type=MESH))
        halo[-1].start()

    relative = jnp.bitwise_and(nb_ref[...] - me * elements + elements, elements * devices - 1)

    def counts(part):
        total = None
        for k in range(4):
            hit = jnp.where(relative[k:k + 1] - part * elements == iota((elements, elements), 0), 1.0, 0.0)
            total = hit if total is None else total + hit
        return total.astype(BF16)

    slot = slot_ref[...].reshape(1, columns)
    dest_row = slot // columns * peer_rows + lax.rem(slot, peer_rows)
    place[...] = ones_where(iota((columns, columns), 0) == dest_row)
    own = mean[...]
    laplace = dot(own, counts(1)) - 4.0 * own
    halo[0].wait()
    halo[1].wait()
    laplace = laplace + (dot(low[...], counts(0)) + dot(high[...], counts(2)))
    spread = ones_where(iota((elements, columns), 0) == iota((elements, columns), 1) // 4)
    flat = flat + DIFFUSION * dot(laplace, spread)
    state[...] = flat.reshape(fields, lev, columns)

    kept = [flat[f * lev:f * lev + zp] for f in range(fields)]
    sent = (kept[0], kept[1]), (kept[2], kept[3] + kept[4] + kept[5])
    for h in range(2):
        fwd_out[h] = dot(place[...], jnp.concatenate(sent[h], axis=0), 1, 1)

    def rows_of(ref, p):
        return ref.at[:, pl.ds(pl.multiple_of(p * peer_rows, peer_rows), peer_rows), :]

    own_fwd = pltpu.make_async_copy(rows_of(fwd_out, me), rows_of(fwd_in, me), fwd_recv.at[0])
    own_fwd.start()

    def send_all(k, _):
        turn = k // per_plane
        to_ga = lax.rem(ga + turn, planes)
        to_dev = lax.rem(dev + k, per_plane)
        pltpu.make_async_remote_copy(
            rows_of(fwd_out, to_ga * per_plane + to_dev), rows_of(fwd_in, me), fwd_send, fwd_recv.at[turn],
            device_id=(to_ga, to_dev), device_id_type=MESH).start()
        return 0
    lax.fori_loop(1, devices, send_all, 0)

    inv = 1.0 / cells
    for c in loads:
        c.wait()

    def widen_block(b, _):
        def widen(z, _):
            for j, (src, dst) in enumerate(((theta_in, th), (water_in, wa))):
                g = src[b, z].astype(F32)
                dst[b, pl.ds(z * cells, cells), :] = g
                s = g[0:ROWS]
                for k in range(1, groups):
                    s = s + g[ROWS * k:ROWS * k + ROWS]
                base[b, j, pl.ds(z, 1), :] = jnp.sum(s, axis=0, keepdims=True) * inv
            return 0
        return lax.fori_loop(0, levels, widen, 0, unroll=2)
    lax.fori_loop(0, planes, widen_block, 0)

    def block(turn, _):
        b = lax.rem(ga - turn + planes, planes)
        here_rows = pl.ds(pl.multiple_of(b * LANES, LANES), LANES)
        arrived = fwd_in.at[:, here_rows, :]
        pltpu.make_async_copy(arrived, arrived, fwd_recv.at[turn]).wait()
        wind = jnp.transpose(fwd_in[0, here_rows, :], (1, 0))
        heat_wet = jnp.transpose(fwd_in[1, here_rows, :], (1, 0))
        heat, wet = heat_wet[:zp], heat_wet[zp:]
        keep_x = 1.0 - 2.0 * X_DIFFUSION
        a = 0.15 * jnp.tanh(wind[:zp])
        m = 0.1 + 0.15 * jax.nn.sigmoid(wind[zp:])
        keep = 1.0 - 2.0 * m
        coef[0] = (X_DIFFUSION - a) / keep_x
        coef[1] = (X_DIFFUSION + a) / keep_x
        coef[2] = keep_x * m
        coef[3] = keep_x * keep
        flag = 0.5 * cloudy_ref[here_rows].astype(F32).reshape(1, LANES)
        flag8 = jnp.broadcast_to(flag, (ROWS, LANES))
        mean_t, mean_w = base[b, 0], base[b, 1]
        condensed = None

        def row(i, z):
            return jnp.broadcast_to(coef[i, pl.ds(z, 1), :], (ROWS, LANES))

        for step in range(SUB):
            first, last = step == 0, step == SUB - 1
            mean_t = mixed(mean_t, m, keep, levels)
            mean_w = mixed(mean_w, m, keep, levels)
            relax_t = RELAX_RATE * (heat - mean_t)
            relax_w = RELAX_RATE * (wet - mean_w)
            coef[4] = relax_t
            coef[5] = relax_w
            coef[6] = relax_w - 0.5 * relax_t - 0.5

            def strip(ref, z, k, strided):
                if strided:
                    return ref.at[b, pl.ds(z * cells + k, ROWS, stride=groups), :]
                return ref.at[b, pl.ds(z * cells + ROWS * k, ROWS), :]

            def advected(z):
                east_c, west_c = row(0, z), row(1, z)
                out = []
                for ref in (th, wa):
                    g = [strip(ref, z, k, first)[...] for k in range(groups)]
                    east = g[1:] + [pltpu.roll(g[0], ROWS - 1, 0)]
                    west = [pltpu.roll(g[-1], 1, 0)] + g[:-1]
                    out.append([g[k] + (east_c * east[k] + west_c * west[k]) for k in range(groups)])
                return out

            def body(z, carry):
                below, here = carry
                above = advected(jnp.minimum(z + 1, levels - 1))
                mz, kz = row(2, z), row(3, z)
                rt, rw, c = row(4, z), row(5, z), row(6, z)
                total = None
                for k in range(groups):
                    t = kz * here[0][k] + mz * (above[0][k] + below[0][k])
                    w = kz * here[1][k] + mz * (above[1][k] + below[1][k])
                    e = flag8 * jnp.maximum((w - 0.5 * t) + c, 0.0)
                    total = e if total is None else total + e
                    strip(th, z, k, last)[...] = (t + rt) + LATENT_HEAT * e
                    strip(wa, z, k, last)[...] = (w + rw) - e
                esum[step, pl.ds(z, 1), :] = jnp.sum(total, axis=0, keepdims=True) * inv
                return here, above

            edge = advected(0)
            lax.fori_loop(0, levels, body, (edge, edge), unroll=2)
            excess = esum[step]
            mean_t = mean_t + relax_t + LATENT_HEAT * excess
            mean_w = mean_w + relax_w - excess
            condensed = excess if condensed is None else condensed + excess

        ret_out[0, here_rows, :] = jnp.transpose(jnp.concatenate([mean_t, mean_w], axis=0), (1, 0))
        ret_out[1, here_rows, :] = jnp.transpose(jnp.concatenate([condensed, condensed], axis=0), (1, 0))

        def answer(k, _):
            to_dev = lax.rem(dev + k, per_plane)
            pltpu.make_async_remote_copy(
                rows_of(ret_out, b * per_plane + to_dev), rows_of(ret_in, me), ret_send, ret_recv,
                device_id=(b, to_dev), device_id_type=MESH).start()
            return 0
        lax.fori_loop(jnp.where(turn == 0, 1, 0), per_plane, answer, 0)

        @pl.when(turn == 0)
        def _():
            pltpu.make_async_copy(rows_of(ret_out, me), rows_of(ret_in, me), ret_recv).start()

        def narrow(z, _):
            for src, dst in ((th, theta_out), (wa, water_out)):
                dst[z, :, here_rows] = src[b, pl.ds(z * cells, cells), :].astype(dst.dtype)
            return 0
        lax.fori_loop(0, levels, narrow, 0, unroll=2)
        return 0
    lax.fori_loop(0, planes, block, 0)

    pltpu.make_async_copy(ret_in, ret_in, ret_recv).wait()
    back = [dot(ret_in[h], place[...], 0, 0) for h in range(2)]
    after = {2: back[0][:zp], 3: back[0][zp:], 4: back[1][:zp]}
    state_out[...] = state[...]
    for f, value in after.items():
        old = state[f, :zp, :]
        new = old + STEP_WEIGHT * (value - old)
        state_out[f, :zp, :] = jnp.where(iota((zp, columns), 0) < levels, new, old)

    others = pl.ds(peer_rows, columns - peer_rows)
    for ref, sem in ((fwd_out, fwd_send), (ret_out, ret_send)):
        gone = ref.at[:, others, :]
        pltpu.make_async_copy(gone, gone, sem).wait()


def on_device(planes, per_plane, column_state, neighbours, crm_slot, cloudy, crm_theta, crm_water):
    fields, lev, columns = column_state.shape
    levels, cells, _ = crm_theta.shape
    zp = -(-levels // ROWS) * ROWS
    elements = columns // 4
    blocks = columns // LANES
    wide = pltpu.VMEM((2, columns, 2 * zp), F32)
    halo = pltpu.VMEM((fields * lev, elements), F32)
    narrow_block = pltpu.VMEM((blocks, levels, cells, LANES), crm_theta.dtype)
    wide_block = pltpu.VMEM((blocks, levels * cells, LANES), F32)
    dma = pltpu.SemaphoreType.DMA
    hbm, vmem = pl.BlockSpec(memory_space=pl.ANY), pl.BlockSpec(memory_space=pltpu.VMEM)
    return pl.pallas_call(
        functools.partial(step_kernel, (planes, per_plane, levels, cells)),
        out_shape=tuple(jax.ShapeDtypeStruct(a.shape, a.dtype) for a in (column_state, crm_theta, crm_water)),
        in_specs=[hbm, vmem, vmem, vmem, hbm, hbm],
        out_specs=(vmem, vmem, vmem),
        scratch_shapes=[
            pltpu.VMEM(column_state.shape, F32), halo, halo, halo, pltpu.VMEM((columns, columns), BF16),
            narrow_block, narrow_block, wide_block, wide_block,
            pltpu.VMEM((7, zp, LANES), F32), pltpu.VMEM((SUB, zp, LANES), F32),
            pltpu.VMEM((blocks, 2, zp, LANES), F32),
            wide, wide, wide, wide,
            dma((1 + 2 * blocks,)), dma((2,)), dma((2,)), dma, dma((planes,)), dma, dma,
        ],
        compiler_params=pltpu.CompilerParams(collective_id=0, has_side_effects=True, vmem_limit_bytes=60 * 2 ** 20),
        name="physics_step",
    )(column_state, neighbours.T, crm_slot, cloudy, crm_theta, crm_water)


def solution(mesh):
    split = ("ga", "dev")
    planes, per_plane = mesh.shape["ga"], mesh.shape["dev"]
    return jax.shard_map(
        functools.partial(on_device, planes, per_plane),
        mesh=mesh,
        in_specs=(P(None, None, split), P(split, None), P(split), P(split), P(None, None, split), P(None, None, split)),
        out_specs=(P(None, None, split), P(None, None, split), P(None, None, split)),
        check_vma=False,
    )
```

```python
import functools

import jax
import jax.numpy as jnp
from jax import lax
from jax.experimental import pallas as pl
from jax.experimental.pallas import tpu as pltpu
from jax.sharding import PartitionSpec as P

SUB = 2
DIFFUSION = 0.15
X_DIFFUSION = 0.2
RELAX_RATE = 0.2
LATENT_HEAT = 0.8
STEP_WEIGHT = 0.5
LANES = 128
ORDER = {4: (2, 1, 3, 0)}
ROWS = 8
MESH = pl.DeviceIdType.MESH
F32, BF16 = jnp.float32, jnp.bfloat16


def pieces(x):
    high = x.astype(BF16)
    rest = x - high.astype(F32)
    middle = rest.astype(BF16)
    return high, middle, (rest - middle.astype(F32)).astype(BF16)


def dot(a, b, left=1, right=0):
    dims = (((left,), (right,)), ((), ()))
    one = functools.partial(lax.dot_general, dimension_numbers=dims, preferred_element_type=F32)
    if a.dtype == BF16:
        parts = [one(a, p) for p in pieces(b)]
    else:
        parts = [one(p, b) for p in pieces(a)]
    return (parts[2] + parts[1]) + parts[0]


def iota(shape, dim):
    return lax.broadcasted_iota(jnp.int32, shape, dim)


def ones_where(mask, value=1.0):
    return jnp.where(mask, value, 0.0).astype(BF16)


def mixed(rows, m, keep, levels):
    up = pltpu.roll(rows, rows.shape[0] - 1, 0)
    down = pltpu.roll(rows, 1, 0)
    z = iota(rows.shape, 0)
    up = jnp.where(z == levels - 1, rows, up)
    down = jnp.where(z == 0, rows, down)
    return keep * rows + m * (up + down)


def step_kernel(sizes, state_hbm, nb_hbm, slot_hbm, cloudy_hbm, theta_hbm, water_hbm,
                state_out, theta_out, water_out,
                nb_ref, slot_ref, cloudy_ref, state, mean, low, high, place, theta_in, water_in, th, wa, coef, esum, base,
                fwd_out, fwd_in, ret_out, ret_in,
                load_sem, halo_send, halo_recv, fwd_send, fwd_recv, ret_send, ret_recv):
    planes, per_plane, levels, cells = sizes
    devices = planes * per_plane
    fields, lev, columns = state.shape
    elements = columns // 4
    peer_rows = columns // devices
    zp = coef.shape[1]
    groups = cells // ROWS
    ga, dev = lax.axis_index("ga"), lax.axis_index("dev")
    me = ga * per_plane + dev

    load_state = pltpu.make_async_copy(state_hbm, state, load_sem.at[0])
    load_state.start()
    small = [pltpu.make_async_copy(src, dst, load_sem.at[1 + 2 * planes + i]) for i, (src, dst) in enumerate(
        ((nb_hbm, nb_ref), (slot_hbm, slot_ref), (cloudy_hbm, cloudy_ref)))]
    for c in small:
        c.start()
    loads = []
    for b in range(planes):
        for j, (src, dst) in enumerate(((theta_hbm, theta_in), (water_hbm, water_in))):
            loads.append(pltpu.make_async_copy(
                src.at[:, :, pl.ds(b * LANES, LANES)], dst.at[b], load_sem.at[1 + 2 * b + j]))
            loads[-1].start()

    barrier = pltpu.get_barrier_semaphore()

    def greet(k, _):
        p = lax.rem(me + k, devices)
        pl.semaphore_signal(barrier, inc=1, device_id=(p // per_plane, lax.rem(p, per_plane)), device_id_type=MESH)
        return 0
    lax.fori_loop(1, devices, greet, 0)

    load_state.wait()
    flat = state[...].reshape(fields * lev, columns)
    gather = ones_where(iota((columns, elements), 0) // 4 == iota((columns, elements), 1), 0.25)
    mean[...] = dot(flat, gather)
    pl.semaphore_wait(barrier, devices - 1)

    halo = []
    for j, (shift, dst) in enumerate(((1, low), (devices - 1, high))):
        p = lax.rem(me + shift, devices)
        halo.append(pltpu.make_async_remote_copy(
            mean, dst, halo_send.at[j], halo_recv.at[j],
            device_id=(p // per_plane, lax.rem(p, per_plane)), device_id_type=MESH))
        halo[-1].start()

    for c in small:
        c.wait()
    relative = jnp.bitwise_and(nb_ref[...] - me * elements + elements, elements * devices - 1)

    def counts(part):
        total = None
        for k in range(4):
            hit = jnp.where(relative[k:k + 1] - part * elements == iota((elements, elements), 0), 1.0, 0.0)
            total = hit if total is None else total + hit
        return total.astype(BF16)

    slot = slot_ref[...].reshape(1, columns)
    dest_row = slot // columns * peer_rows + lax.rem(slot, peer_rows)
    place[...] = ones_where(iota((columns, columns), 0) == dest_row)
    own = mean[...]
    laplace = dot(own, counts(1)) - 4.0 * own
    halo[0].wait()
    halo[1].wait()
    laplace = laplace + (dot(low[...], counts(0)) + dot(high[...], counts(2)))
    spread = ones_where(iota((elements, columns), 0) == iota((elements, columns), 1) // 4)
    flat = flat + DIFFUSION * dot(laplace, spread)
    state[...] = flat.reshape(fields, lev, columns)

    kept = [flat[f * lev:f * lev + zp] for f in range(fields)]
    sent = (kept[0], kept[1]), (kept[2], kept[3] + kept[4] + kept[5])
    for h in range(2):
        fwd_out[h] = dot(place[...], jnp.concatenate(sent[h], axis=0), 1, 1)

    def rows_of(ref, p):
        return ref.at[:, pl.ds(pl.multiple_of(p * peer_rows, peer_rows), peer_rows), :]

    own_fwd = pltpu.make_async_copy(rows_of(fwd_out, me), rows_of(fwd_in, me), fwd_recv.at[planes - 1])
    own_fwd.start()

    def ahead(turn):
        out = (turn * 0)
        for t, far in enumerate(ORDER[planes]):
            out = jnp.where(turn == t, far, out)
        return out

    def send_all(k, _):
        turn = k // per_plane
        to_ga = lax.rem(ga - ahead(turn) + planes, planes)
        to_dev = lax.rem(dev + k + 1, per_plane)
        pltpu.make_async_remote_copy(
            rows_of(fwd_out, to_ga * per_plane + to_dev), rows_of(fwd_in, me), fwd_send, fwd_recv.at[turn],
            device_id=(to_ga, to_dev), device_id_type=MESH).start()
        return 0
    lax.fori_loop(0, devices - 1, send_all, 0)

    inv = 1.0 / cells
    for c in loads:
        c.wait()

    def widen_block(b, _):
        def widen(z, _):
            for j, (src, dst) in enumerate(((theta_in, th), (water_in, wa))):
                g = src[b, z].astype(F32)
                dst[b, pl.ds(z * cells, cells), :] = g
                s = g[0:ROWS]
                for k in range(1, groups):
                    s = s + g[ROWS * k:ROWS * k + ROWS]
                base[b, j, pl.ds(z, 1), :] = jnp.sum(s, axis=0, keepdims=True) * inv
            return 0
        return lax.fori_loop(0, levels, widen, 0, unroll=2)
    lax.fori_loop(0, planes, widen_block, 0)

    def block(turn, _):
        b = lax.rem(ga + ahead(turn), planes)
        here_rows = pl.ds(pl.multiple_of(b * LANES, LANES), LANES)
        arrived = fwd_in.at[:, here_rows, :]
        pltpu.make_async_copy(arrived, arrived, fwd_recv.at[turn]).wait()
        wind = jnp.transpose(fwd_in[0, here_rows, :], (1, 0))
        heat_wet = jnp.transpose(fwd_in[1, here_rows, :], (1, 0))
        heat, wet = heat_wet[:zp], heat_wet[zp:]
        keep_x = 1.0 - 2.0 * X_DIFFUSION
        a = 0.15 * jnp.tanh(wind[:zp])
        m = 0.1 + 0.15 * jax.nn.sigmoid(wind[zp:])
        keep = 1.0 - 2.0 * m
        coef[0] = (X_DIFFUSION - a) / keep_x
        coef[1] = (X_DIFFUSION + a) / keep_x
        coef[2] = keep_x * m
        coef[3] = keep_x * keep
        flag = 0.5 * cloudy_ref[here_rows].astype(F32).reshape(1, LANES)
        flag8 = jnp.broadcast_to(flag, (ROWS, LANES))
        mean_t, mean_w = base[b, 0], base[b, 1]
        condensed = None

        def row(i, z):
            return jnp.broadcast_to(coef[i, pl.ds(z, 1), :], (ROWS, LANES))

        for step in range(SUB):
            first, last = step == 0, step == SUB - 1
            mean_t = mixed(mean_t, m, keep, levels)
            mean_w = mixed(mean_w, m, keep, levels)
            relax_t = RELAX_RATE * (heat - mean_t)
            relax_w = RELAX_RATE * (wet - mean_w)
            coef[4] = relax_t
            coef[5] = relax_w
            coef[6] = relax_w - 0.5 * relax_t - 0.5

            def strip(ref, z, k, strided):
                if strided:
                    return ref.at[b, pl.ds(z * cells + k, ROWS, stride=groups), :]
                return ref.at[b, pl.ds(z * cells + ROWS * k, ROWS), :]

            def advected(z):
                east_c, west_c = row(0, z), row(1, z)
                out = []
                for ref in (th, wa):
                    g = [strip(ref, z, k, first)[...] for k in range(groups)]
                    east = g[1:] + [pltpu.roll(g[0], ROWS - 1, 0)]
                    west = [pltpu.roll(g[-1], 1, 0)] + g[:-1]
                    out.append([g[k] + (east_c * east[k] + west_c * west[k]) for k in range(groups)])
                return out

            def body(z, carry):
                below, here = carry
                above = advected(jnp.minimum(z + 1, levels - 1))
                mz, kz = row(2, z), row(3, z)
                rt, rw, c = row(4, z), row(5, z), row(6, z)
                total = None
                for k in range(groups):
                    t = kz * here[0][k] + mz * (above[0][k] + below[0][k])
                    w = kz * here[1][k] + mz * (above[1][k] + below[1][k])
                    e = flag8 * jnp.maximum((w - 0.5 * t) + c, 0.0)
                    total = e if total is None else total + e
                    strip(th, z, k, last)[...] = (t + rt) + LATENT_HEAT * e
                    strip(wa, z, k, last)[...] = (w + rw) - e
                esum[step, pl.ds(z, 1), :] = jnp.sum(total, axis=0, keepdims=True) * inv
                return here, above

            edge = advected(0)
            lax.fori_loop(0, levels, body, (edge, edge), unroll=2)
            excess = esum[step]
            mean_t = mean_t + relax_t + LATENT_HEAT * excess
            mean_w = mean_w + relax_w - excess
            condensed = excess if condensed is None else condensed + excess

        ret_out[0, here_rows, :] = jnp.transpose(jnp.concatenate([mean_t, mean_w], axis=0), (1, 0))
        ret_out[1, here_rows, :] = jnp.transpose(jnp.concatenate([condensed, condensed], axis=0), (1, 0))

        def answer(k, _):
            to_dev = lax.rem(dev + k, per_plane)
            pltpu.make_async_remote_copy(
                rows_of(ret_out, b * per_plane + to_dev), rows_of(ret_in, me), ret_send, ret_recv,
                device_id=(b, to_dev), device_id_type=MESH).start()
            return 0
        lax.fori_loop(jnp.where(turn == planes - 1, 1, 0), per_plane, answer, 0)

        @pl.when(turn == planes - 1)
        def _():
            pltpu.make_async_copy(rows_of(ret_out, me), rows_of(ret_in, me), ret_recv).start()

        def narrow(z, _):
            for src, dst in ((th, theta_out), (wa, water_out)):
                dst[z, :, here_rows] = src[b, pl.ds(z * cells, cells), :].astype(dst.dtype)
            return 0
        lax.fori_loop(0, levels, narrow, 0, unroll=2)
        return 0
    lax.fori_loop(0, planes, block, 0)

    pltpu.make_async_copy(ret_in, ret_in, ret_recv).wait()
    back = [dot(ret_in[h], place[...], 0, 0) for h in range(2)]
    after = {2: back[0][:zp], 3: back[0][zp:], 4: back[1][:zp]}
    state_out[...] = state[...]
    for f, value in after.items():
        old = state[f, :zp, :]
        new = old + STEP_WEIGHT * (value - old)
        state_out[f, :zp, :] = jnp.where(iota((zp, columns), 0) < levels, new, old)

    others = pl.ds(peer_rows, columns - peer_rows)
    for ref, sem in ((fwd_out, fwd_send), (ret_out, ret_send)):
        gone = ref.at[:, others, :]
        pltpu.make_async_copy(gone, gone, sem).wait()


def store_kernel(*refs):
    sems = refs[6]
    copies = [pltpu.make_async_copy(refs[i], refs[3 + i], sems.at[i]) for i in range(3)]
    for c in copies:
        c.start()
    for c in copies:
        c.wait()


def on_device(planes, per_plane, column_state, neighbours, crm_slot, cloudy, crm_theta, crm_water):
    fields, lev, columns = column_state.shape
    levels, cells, _ = crm_theta.shape
    zp = -(-levels // ROWS) * ROWS
    elements = columns // 4
    blocks = columns // LANES
    wide = pltpu.VMEM((2, columns, 2 * zp), F32)
    halo = pltpu.VMEM((fields * lev, elements), F32)
    narrow_block = pltpu.VMEM((blocks, levels, cells, LANES), crm_theta.dtype)
    wide_block = pltpu.VMEM((blocks, levels * cells, LANES), F32)
    dma = pltpu.SemaphoreType.DMA
    hbm, vmem = pl.BlockSpec(memory_space=pl.ANY), pl.BlockSpec(memory_space=pltpu.VMEM)
    inputs = [pltpu.with_memory_space_constraint(a, pltpu.HBM)
              for a in (column_state, neighbours.T, crm_slot, cloudy, crm_theta, crm_water)]
    results = pl.pallas_call(
        functools.partial(step_kernel, (planes, per_plane, levels, cells)),
        out_shape=tuple(jax.ShapeDtypeStruct(a.shape, a.dtype) for a in (column_state, crm_theta, crm_water)),
        in_specs=[hbm] * 6,
        out_specs=(vmem, vmem, vmem),
        scratch_shapes=[
            pltpu.VMEM((4, elements), jnp.int32), pltpu.VMEM((columns,), jnp.int32), pltpu.VMEM((columns,), jnp.int32),
            pltpu.VMEM(column_state.shape, F32), halo, halo, halo, pltpu.VMEM((columns, columns), BF16),
            narrow_block, narrow_block, wide_block, wide_block,
            pltpu.VMEM((7, zp, LANES), F32), pltpu.VMEM((SUB, zp, LANES), F32),
            pltpu.VMEM((blocks, 2, zp, LANES), F32),
            wide, wide, wide, wide,
            dma((4 + 2 * blocks,)), dma((2,)), dma((2,)), dma, dma((planes,)), dma, dma,
        ],
        compiler_params=pltpu.CompilerParams(collective_id=0, has_side_effects=True, vmem_limit_bytes=28 * 2 ** 20),
        name="physics_step",
    )(*inputs)
    return pl.pallas_call(
        store_kernel,
        out_shape=tuple(jax.ShapeDtypeStruct(a.shape, a.dtype) for a in results),
        in_specs=[vmem] * 3,
        out_specs=(hbm, hbm, hbm),
        scratch_shapes=[dma((3,))],
        compiler_params=pltpu.CompilerParams(vmem_limit_bytes=16 * 2 ** 20),
        name="store",
    )(*results)


def solution(mesh):
    split = ("ga", "dev")
    planes, per_plane = mesh.shape["ga"], mesh.shape["dev"]
    return jax.shard_map(
        functools.partial(on_device, planes, per_plane),
        mesh=mesh,
        in_specs=(P(None, None, split), P(split, None), P(split), P(split), P(None, None, split), P(None, None, split)),
        out_specs=(P(None, None, split), P(None, None, split), P(None, None, split)),
        check_vma=False,
    )
```

```python
import functools

import jax
import jax.numpy as jnp
from jax import lax
from jax.experimental import pallas as pl
from jax.experimental.pallas import tpu as pltpu
from jax.sharding import PartitionSpec as P

SUB = 2
DIFFUSION = 0.15
X_DIFFUSION = 0.2
RELAX_RATE = 0.2
LATENT_HEAT = 0.8
STEP_WEIGHT = 0.5
LANES = 128
ORDER = {4: (2, 1, 3, 0)}
ROWS = 8
MESH = pl.DeviceIdType.MESH
F32, BF16 = jnp.float32, jnp.bfloat16


def pieces(x):
    high = x.astype(BF16)
    return high, (x - high.astype(F32)).astype(BF16)


def dot(a, b, left=1, right=0):
    dims = (((left,), (right,)), ((), ()))
    one = functools.partial(lax.dot_general, dimension_numbers=dims, preferred_element_type=F32)
    if a.dtype == BF16:
        parts = [one(a, p) for p in pieces(b)]
    else:
        parts = [one(p, b) for p in pieces(a)]
    return parts[1] + parts[0]


def iota(shape, dim):
    return lax.broadcasted_iota(jnp.int32, shape, dim)


def ones_where(mask, value=1.0):
    return jnp.where(mask, value, 0.0).astype(BF16)


def neighbours_of(g):
    east = g[1:] + [pltpu.roll(g[0], ROWS - 1, 0)]
    west = [pltpu.roll(g[-1], 1, 0)] + g[:-1]
    return east, west


def mixed(rows, m, keep, levels):
    up = pltpu.roll(rows, rows.shape[0] - 1, 0)
    down = pltpu.roll(rows, 1, 0)
    z = iota(rows.shape, 0)
    up = jnp.where(z == levels - 1, rows, up)
    down = jnp.where(z == 0, rows, down)
    return keep * rows + m * (up + down)


def step_kernel(sizes, state_hbm, nb_hbm, slot_hbm, cloudy_hbm, theta_hbm, water_hbm,
                state_out, theta_out, water_out,
                nb_ref, slot_ref, cloudy_ref, state, mean, low, high, place, theta_in, water_in, even_t, odd_t, even_p, odd_p, coef, sums,
                fwd_out, fwd_in, ret_out, ret_in,
                load_sem, halo_send, halo_recv, fwd_send, fwd_recv, ret_send, ret_recv):
    planes, per_plane, levels, cells = sizes
    devices = planes * per_plane
    fields, lev, columns = state.shape
    elements = columns // 4
    peer_rows = columns // devices
    zp = coef.shape[1]
    groups = cells // ROWS
    ga, dev = lax.axis_index("ga"), lax.axis_index("dev")
    me = ga * per_plane + dev
    keep_x = 1.0 - 2.0 * X_DIFFUSION
    side = X_DIFFUSION / keep_x

    load_state = pltpu.make_async_copy(state_hbm, state, load_sem.at[0])
    load_state.start()
    small = [pltpu.make_async_copy(src, dst, load_sem.at[1 + 2 * planes + i]) for i, (src, dst) in enumerate(
        ((nb_hbm, nb_ref), (slot_hbm, slot_ref), (cloudy_hbm, cloudy_ref)))]
    for c in small:
        c.start()
    loads = []
    for b in range(planes):
        for j, (src, dst) in enumerate(((theta_hbm, theta_in), (water_hbm, water_in))):
            loads.append(pltpu.make_async_copy(
                src.at[:, :, pl.ds(b * LANES, LANES)], dst.at[b], load_sem.at[1 + 2 * b + j]))
            loads[-1].start()

    barrier = pltpu.get_barrier_semaphore()

    for far in ORDER[planes]:
        to_ga = lax.rem(ga + far, planes)

        def greet(k, _):
            pl.semaphore_signal(barrier, inc=1, device_id=(to_ga, jnp.bitwise_xor(dev, k)), device_id_type=MESH)
            return 0
        lax.fori_loop(0 if far else 1, per_plane, greet, 0)

    load_state.wait()
    flat = state[...].reshape(fields * lev, columns)
    gather = ones_where(iota((columns, elements), 0) // 4 == iota((columns, elements), 1), 0.25)
    mean[...] = dot(flat, gather)
    pl.semaphore_wait(barrier, devices - 1)

    halo = []
    for j, (shift, dst) in enumerate(((1, low), (devices - 1, high))):
        p = lax.rem(me + shift, devices)
        halo.append(pltpu.make_async_remote_copy(
            mean, dst, halo_send.at[j], halo_recv.at[j],
            device_id=(p // per_plane, lax.rem(p, per_plane)), device_id_type=MESH))
        halo[-1].start()

    for c in small:
        c.wait()
    relative = jnp.bitwise_and(nb_ref[...] - me * elements + elements, elements * devices - 1)

    def counts(part):
        total = None
        for k in range(4):
            hit = jnp.where(relative[k:k + 1] - part * elements == iota((elements, elements), 0), 1.0, 0.0)
            total = hit if total is None else total + hit
        return total.astype(BF16)

    slot = slot_ref[...].reshape(1, columns)
    dest_row = slot // columns * peer_rows + lax.rem(slot, peer_rows)
    place[...] = ones_where(iota((columns, columns), 0) == dest_row)
    own = mean[...]
    laplace = dot(own, counts(1)) - 4.0 * own
    inv = 1.0 / cells
    for c in loads:
        c.wait()

    def widen(i, _):
        b, pair = i // (levels // 2), lax.rem(i, levels // 2)
        for j in range(2):
            z = 2 * pair + j
            half = 0.5 * theta_in[b, z].astype(F32)
            gap = (water_in[b, z].astype(F32) - half) - 0.5
            for part, (dst, g) in enumerate(((even_t, half), (even_p, gap))):
                dst[b, pl.ds(z * cells, cells), :] = g
                sums[part, b, pl.ds(z * ROWS, ROWS), :] = functools.reduce(
                    jnp.add, [g[ROWS * k:ROWS * k + ROWS] for k in range(groups)])
        return 0
    lax.fori_loop(0, planes * levels // 2, widen, 0)

    def slopes(i, _):
        b, pair = i // (levels // 2), lax.rem(i, levels // 2)
        for j in range(2):
            z = 2 * pair + j
            for even, odd in ((even_t, odd_t), (even_p, odd_p)):
                g = [even[b, pl.ds(z * cells + k, ROWS, stride=groups), :] for k in range(groups)]
                east, west = neighbours_of(g)
                for k in range(groups):
                    at = pl.ds(z * cells + ROWS * k, ROWS)
                    even[b, at, :] = g[k] + side * (east[k] + west[k])
                    odd[b, at, :] = east[k] - west[k]
        return 0

    def total_of(part, b):
        rows = [sums[part, b, pl.ds(k, zp, stride=ROWS), :] for k in range(ROWS)]
        return functools.reduce(jnp.add, rows) * inv

    halo[0].wait()
    halo[1].wait()
    laplace = laplace + (dot(low[...], counts(0)) + dot(high[...], counts(2)))
    spread = ones_where(iota((elements, columns), 0) == iota((elements, columns), 1) // 4)
    flat = flat + DIFFUSION * dot(laplace, spread)
    state[...] = flat.reshape(fields, lev, columns)

    kept = [flat[f * lev:f * lev + zp] for f in range(fields)]
    sent = (kept[0], kept[1]), (kept[2], kept[3] + kept[4] + kept[5])
    for h in range(2):
        fwd_out[h] = dot(place[...], jnp.concatenate(sent[h], axis=0), 1, 1)

    def rows_of(ref, p):
        return ref.at[:, pl.ds(pl.multiple_of(p * peer_rows, peer_rows), peer_rows), :]

    own_fwd = pltpu.make_async_copy(rows_of(fwd_out, me), rows_of(fwd_in, me), fwd_recv.at[planes - 1])
    own_fwd.start()

    def ahead(turn):
        out = (turn * 0)
        for t, far in enumerate(ORDER[planes]):
            out = jnp.where(turn == t, far, out)
        return out

    for turn, far in enumerate(ORDER[planes]):
        to_ga = lax.rem(ga + (planes - far), planes)

        def send(k, _):
            to_dev = jnp.bitwise_xor(dev, k)
            pltpu.make_async_remote_copy(
                rows_of(fwd_out, to_ga * per_plane + to_dev), rows_of(fwd_in, me), fwd_send, fwd_recv.at[turn],
                device_id=(to_ga, to_dev), device_id_type=MESH).start()
            return 0
        lax.fori_loop(0 if far else 1, per_plane, send, 0)

    lax.fori_loop(0, planes * levels // 2, slopes, 0)

    def block(turn, _):
        b = lax.rem(ga + ahead(turn), planes)
        here_rows = pl.ds(pl.multiple_of(b * LANES, LANES), LANES)
        arrived = fwd_in.at[:, here_rows, :]
        pltpu.make_async_copy(arrived, arrived, fwd_recv.at[turn]).wait()
        wind = jnp.transpose(fwd_in[0, here_rows, :], (1, 0))
        heat_wet = jnp.transpose(fwd_in[1, here_rows, :], (1, 0))
        heat, wet = heat_wet[:zp], heat_wet[zp:]
        slope = (0.15 / keep_x) * jnp.tanh(wind[:zp])
        m = 0.1 + 0.15 * jax.nn.sigmoid(wind[zp:])
        keep = 1.0 - 2.0 * m
        coef[0] = slope
        coef[1] = side - slope
        coef[2] = side + slope
        coef[3] = keep_x * m
        coef[4] = keep_x * keep
        flag = cloudy_ref[here_rows].astype(F32).reshape(1, LANES)
        dry = jnp.broadcast_to((0.5 + 0.25 * LATENT_HEAT) * flag, (ROWS, LANES))
        warm = jnp.broadcast_to((0.25 * LATENT_HEAT) * flag, (ROWS, LANES))
        mean_t, mean_p = total_of(0, b), total_of(1, b)
        aim_t = 0.5 * heat
        aim_p = (wet - aim_t) - 0.5
        row_t = row_p = condensed = None

        def row(i, z):
            return jnp.broadcast_to(coef[i, pl.ds(z, 1), :], (ROWS, LANES))

        for step in range(SUB):
            first, last = step == 0, step == SUB - 1
            mean_t = mixed(mean_t, m, keep, levels)
            mean_p = mixed(mean_p, m, keep, levels)
            relax_t = RELAX_RATE * (aim_t - mean_t)
            relax_p = RELAX_RATE * (aim_p - mean_p)
            row_t = relax_t if first else mixed(row_t, m, keep, levels) + relax_t
            row_p = relax_p if first else mixed(row_p, m, keep, levels) + relax_p
            coef[5] = row_p

            def strip(ref, z, k, strided):
                if strided:
                    return ref.at[b, pl.ds(z * cells + k, ROWS, stride=groups), :]
                return ref.at[b, pl.ds(z * cells + ROWS * k, ROWS), :]

            def advected(z):
                if first:
                    rate = row(0, z)
                    return [[strip(even, z, k, False)[...] - rate * strip(odd, z, k, False)[...] for k in range(groups)]
                            for even, odd in ((even_t, odd_t), (even_p, odd_p))]
                east_c, west_c = row(1, z), row(2, z)
                out = []
                for ref in (even_t, even_p):
                    g = [strip(ref, z, k, False)[...] for k in range(groups)]
                    east, west = neighbours_of(g)
                    out.append([g[k] + (east_c * east[k] + west_c * west[k]) for k in range(groups)])
                return out

            def body(z, carry):
                below, here = carry
                above = advected(jnp.minimum(z + 1, levels - 1))
                mz, kz, offset = row(3, z), row(4, z), row(5, z)
                total = None
                for k in range(groups):
                    t = kz * here[0][k] + mz * (above[0][k] + below[0][k])
                    p = kz * here[1][k] + mz * (above[1][k] + below[1][k])
                    e = jnp.maximum(p + offset, 0.0)
                    total = e if total is None else total + e
                    strip(odd_t if last else even_t, z, k, last)[...] = t + warm * e
                    strip(odd_p if last else even_p, z, k, last)[...] = p - dry * e
                sums[step, b, pl.ds(z * ROWS, ROWS), :] = total
                return here, above

            edge = advected(0)
            lax.fori_loop(0, levels, body, (edge, edge), unroll=2)
            excess = (0.5 * flag) * total_of(step, b)
            mean_t = mean_t + relax_t + (0.5 * LATENT_HEAT) * excess
            mean_p = mean_p + relax_p - (1.0 + 0.5 * LATENT_HEAT) * excess
            condensed = excess if condensed is None else condensed + excess

        coef[5] = row_t + row_t
        coef[6] = (row_p + row_t) + 0.5
        mean_w = (mean_p + mean_t) + 0.5
        mean_t = mean_t + mean_t

        ret_out[0, here_rows, :] = jnp.transpose(jnp.concatenate([mean_t, mean_w], axis=0), (1, 0))
        ret_out[1, here_rows, :] = jnp.transpose(jnp.concatenate([condensed, condensed], axis=0), (1, 0))

        def answer(k, _):
            to_dev = jnp.bitwise_xor(dev, k)
            pltpu.make_async_remote_copy(
                rows_of(ret_out, b * per_plane + to_dev), rows_of(ret_in, me), ret_send, ret_recv,
                device_id=(b, to_dev), device_id_type=MESH).start()
            return 0
        lax.fori_loop(jnp.where(turn == planes - 1, 1, 0), per_plane, answer, 0)

        @pl.when(turn == planes - 1)
        def _():
            pltpu.make_async_copy(rows_of(ret_out, me), rows_of(ret_in, me), ret_recv).start()

        def narrow(z, _):
            at = pl.ds(z * cells, cells)
            half, gap = odd_t[b, at, :], odd_p[b, at, :]
            add_t, add_w = (jnp.broadcast_to(coef[i, pl.ds(z, 1), :], (cells, LANES)) for i in (5, 6))
            theta_out[z, :, here_rows] = ((half + half) + add_t).astype(theta_out.dtype)
            water_out[z, :, here_rows] = ((gap + half) + add_w).astype(water_out.dtype)
            return 0
        lax.fori_loop(0, levels, narrow, 0, unroll=2)
        return 0
    lax.fori_loop(0, planes, block, 0)

    pltpu.make_async_copy(ret_in, ret_in, ret_recv).wait()
    back = [dot(ret_in[h], place[...], 0, 0) for h in range(2)]
    after = {2: back[0][:zp], 3: back[0][zp:], 4: back[1][:zp]}
    state_out[...] = state[...]
    for f, value in after.items():
        old = state[f, :zp, :]
        new = old + STEP_WEIGHT * (value - old)
        state_out[f, :zp, :] = jnp.where(iota((zp, columns), 0) < levels, new, old)

    others = pl.ds(peer_rows, columns - peer_rows)
    for ref, sem in ((fwd_out, fwd_send), (ret_out, ret_send)):
        gone = ref.at[:, others, :]
        pltpu.make_async_copy(gone, gone, sem).wait()


def store_kernel(*refs):
    sems = refs[6]
    copies = [pltpu.make_async_copy(refs[i], refs[3 + i], sems.at[i]) for i in range(3)]
    for c in copies:
        c.start()
    for c in copies:
        c.wait()


def on_device(planes, per_plane, column_state, neighbours, crm_slot, cloudy, crm_theta, crm_water):
    fields, lev, columns = column_state.shape
    levels, cells, _ = crm_theta.shape
    zp = -(-levels // ROWS) * ROWS
    elements = columns // 4
    blocks = columns // LANES
    wide = pltpu.VMEM((2, columns, 2 * zp), F32)
    halo = pltpu.VMEM((fields * lev, elements), F32)
    narrow_block = pltpu.VMEM((blocks, levels, cells, LANES), crm_theta.dtype)
    wide_block = pltpu.VMEM((blocks, levels * cells, LANES), F32)
    dma = pltpu.SemaphoreType.DMA
    hbm, vmem = pl.BlockSpec(memory_space=pl.ANY), pl.BlockSpec(memory_space=pltpu.VMEM)
    inputs = [pltpu.with_memory_space_constraint(a, pltpu.HBM)
              for a in (column_state, neighbours.T, crm_slot, cloudy, crm_theta, crm_water)]
    results = pl.pallas_call(
        functools.partial(step_kernel, (planes, per_plane, levels, cells)),
        out_shape=tuple(jax.ShapeDtypeStruct(a.shape, a.dtype) for a in (column_state, crm_theta, crm_water)),
        in_specs=[hbm] * 6,
        out_specs=(vmem, vmem, vmem),
        scratch_shapes=[
            pltpu.VMEM((4, elements), jnp.int32), pltpu.VMEM((columns,), jnp.int32), pltpu.VMEM((columns,), jnp.int32),
            pltpu.VMEM(column_state.shape, F32), halo, halo, halo, pltpu.VMEM((columns, columns), BF16),
            narrow_block, narrow_block, wide_block, wide_block, wide_block, wide_block,
            pltpu.VMEM((7, zp, LANES), F32), pltpu.VMEM((2, blocks, zp * ROWS, LANES), F32),
            wide, wide, wide, wide,
            dma((4 + 2 * blocks,)), dma((2,)), dma((2,)), dma, dma((planes,)), dma, dma,
        ],
        compiler_params=pltpu.CompilerParams(collective_id=0, has_side_effects=True, vmem_limit_bytes=36 * 2 ** 20),
        name="physics_step",
    )(*inputs)
    return pl.pallas_call(
        store_kernel,
        out_shape=tuple(jax.ShapeDtypeStruct(a.shape, a.dtype) for a in results),
        in_specs=[vmem] * 3,
        out_specs=(hbm, hbm, hbm),
        scratch_shapes=[dma((3,))],
        compiler_params=pltpu.CompilerParams(vmem_limit_bytes=16 * 2 ** 20),
        name="store",
    )(*results)


def solution(mesh):
    split = ("ga", "dev")
    planes, per_plane = mesh.shape["ga"], mesh.shape["dev"]
    return jax.shard_map(
        functools.partial(on_device, planes, per_plane),
        mesh=mesh,
        in_specs=(P(None, None, split), P(split, None), P(split), P(split), P(None, None, split), P(None, None, split)),
        out_specs=(P(None, None, split), P(None, None, split), P(None, None, split)),
        check_vma=False,
    )
```

```python
import functools

import jax
import jax.numpy as jnp
from jax import lax
from jax.experimental import pallas as pl
from jax.experimental.pallas import tpu as pltpu
from jax.sharding import PartitionSpec as P

SUB = 2
DIFFUSION = 0.15
X_DIFFUSION = 0.2
RELAX_RATE = 0.2
LATENT_HEAT = 0.8
DRYING = 1.0 + 0.5 * LATENT_HEAT
STEP_WEIGHT = 0.5
LANES = 128
ORDER = {4: (2, 1, 3, 0)}
ROWS = 8
MESH = pl.DeviceIdType.MESH
F32, BF16 = jnp.float32, jnp.bfloat16


def pieces(x):
    high = x.astype(BF16)
    return high, (x - high.astype(F32)).astype(BF16)


def dot(a, b, left=1, right=0):
    dims = (((left,), (right,)), ((), ()))
    one = functools.partial(lax.dot_general, dimension_numbers=dims, preferred_element_type=F32)
    if a.dtype == BF16:
        parts = [one(a, p) for p in pieces(b)]
    else:
        parts = [one(p, b) for p in pieces(a)]
    return parts[1] + parts[0]


def iota(shape, dim):
    return lax.broadcasted_iota(jnp.int32, shape, dim)


def ones_where(mask, value=1.0):
    return jnp.where(mask, value, 0.0).astype(BF16)


def neighbours_of(g):
    east = g[1:] + [pltpu.roll(g[0], ROWS - 1, 0)]
    west = [pltpu.roll(g[-1], 1, 0)] + g[:-1]
    return east, west


def mixed(rows, m, keep, levels):
    up = pltpu.roll(rows, rows.shape[0] - 1, 0)
    down = pltpu.roll(rows, 1, 0)
    z = iota(rows.shape, 0)
    up = jnp.where(z == levels - 1, rows, up)
    down = jnp.where(z == 0, rows, down)
    return keep * rows + m * (up + down)


def step_kernel(sizes, state_hbm, nb_hbm, slot_hbm, cloudy_hbm, theta_hbm, water_hbm,
                state_out, theta_out, water_out,
                nb_ref, slot_ref, cloudy_ref, state, mean, low, high, place, theta_in, water_in, even_p, odd_p, even_c, odd_c, half_way, coef, sums,
                fwd_out, fwd_in, ret_out, ret_in,
                load_sem, halo_send, halo_recv, fwd_send, fwd_recv, ret_send, ret_recv):
    planes, per_plane, levels, cells = sizes
    devices = planes * per_plane
    fields, lev, columns = state.shape
    elements = columns // 4
    peer_rows = columns // devices
    zp = coef.shape[2]
    groups = cells // ROWS
    ga, dev = lax.axis_index("ga"), lax.axis_index("dev")
    me = ga * per_plane + dev
    keep_x = 1.0 - 2.0 * X_DIFFUSION
    side = X_DIFFUSION / keep_x

    load_state = pltpu.make_async_copy(state_hbm, state, load_sem.at[0])
    load_state.start()
    small = [pltpu.make_async_copy(src, dst, load_sem.at[1 + 2 * planes + i]) for i, (src, dst) in enumerate(
        ((nb_hbm, nb_ref), (slot_hbm, slot_ref), (cloudy_hbm, cloudy_ref)))]
    for c in small:
        c.start()
    loads = []
    for b in range(planes):
        for j, (src, dst) in enumerate(((theta_hbm, theta_in), (water_hbm, water_in))):
            loads.append(pltpu.make_async_copy(
                src.at[:, :, pl.ds(b * LANES, LANES)], dst.at[b], load_sem.at[1 + 2 * b + j]))
            loads[-1].start()

    barrier = pltpu.get_barrier_semaphore()

    for far in ORDER[planes]:
        to_ga = lax.rem(ga + far, planes)

        def greet(k, _):
            pl.semaphore_signal(barrier, inc=1, device_id=(to_ga, jnp.bitwise_xor(dev, k)), device_id_type=MESH)
            return 0
        lax.fori_loop(0 if far else 1, per_plane, greet, 0)

    load_state.wait()
    flat = state[...].reshape(fields * lev, columns)
    gather = ones_where(iota((columns, elements), 0) // 4 == iota((columns, elements), 1), 0.25)
    mean[...] = dot(flat, gather)
    pl.semaphore_wait(barrier, devices - 1)

    halo = []
    for j, (shift, dst) in enumerate(((1, low), (devices - 1, high))):
        p = lax.rem(me + shift, devices)
        halo.append(pltpu.make_async_remote_copy(
            mean, dst, halo_send.at[j], halo_recv.at[j],
            device_id=(p // per_plane, lax.rem(p, per_plane)), device_id_type=MESH))
        halo[-1].start()

    for c in small:
        c.wait()
    relative = jnp.bitwise_and(nb_ref[...] - me * elements + elements, elements * devices - 1)

    def counts(part):
        total = None
        for k in range(4):
            hit = jnp.where(relative[k:k + 1] - part * elements == iota((elements, elements), 0), 1.0, 0.0)
            total = hit if total is None else total + hit
        return total.astype(BF16)

    slot = slot_ref[...].reshape(1, columns)
    dest_row = slot // columns * peer_rows + lax.rem(slot, peer_rows)
    place[...] = ones_where(iota((columns, columns), 0) == dest_row)
    own = mean[...]
    laplace = dot(own, counts(1)) - 4.0 * own
    inv = 1.0 / cells
    for c in loads:
        c.wait()

    def widen(i, _):
        b, pair = i // (levels // 2), lax.rem(i, levels // 2)
        for j in range(2):
            z = 2 * pair + j
            warmth, wetness = theta_in[b, z].astype(F32), water_in[b, z].astype(F32)
            gap = (wetness - 0.5 * warmth) - 0.5
            for part, (dst, g) in enumerate(((even_p, gap), (even_c, warmth + LATENT_HEAT * wetness))):
                dst[b, pl.ds(z * cells, cells), :] = g
                sums[part, b, pl.ds(z * ROWS, ROWS), :] = functools.reduce(
                    jnp.add, [g[ROWS * k:ROWS * k + ROWS] for k in range(groups)])
        return 0
    lax.fori_loop(0, planes * levels // 2, widen, 0, unroll=4)

    def slopes(i, _):
        b, pair = i // (levels // 2), lax.rem(i, levels // 2)
        for j in range(2):
            z = 2 * pair + j
            for even, odd in ((even_p, odd_p), (even_c, odd_c)):
                g = [even[b, pl.ds(z * cells + k, ROWS, stride=groups), :] for k in range(groups)]
                east, west = neighbours_of(g)
                for k in range(groups):
                    at = pl.ds(z * cells + ROWS * k, ROWS)
                    even[b, at, :] = g[k] + side * (east[k] + west[k])
                    odd[b, at, :] = east[k] - west[k]
        return 0

    def total_of(part, b):
        rows = [sums[part, b, pl.ds(k, zp, stride=ROWS), :] for k in range(ROWS)]
        return functools.reduce(jnp.add, rows) * inv

    halo[0].wait()
    halo[1].wait()
    laplace = laplace + (dot(low[...], counts(0)) + dot(high[...], counts(2)))
    spread = ones_where(iota((elements, columns), 0) == iota((elements, columns), 1) // 4)
    flat = flat + DIFFUSION * dot(laplace, spread)
    state[...] = flat.reshape(fields, lev, columns)

    kept = [flat[f * lev:f * lev + zp] for f in range(fields)]
    sent = (kept[0], kept[1]), (kept[2], kept[3] + kept[4] + kept[5])
    for h in range(2):
        fwd_out[h] = dot(place[...], jnp.concatenate(sent[h], axis=0), 1, 1)

    def rows_of(ref, p):
        return ref.at[:, pl.ds(pl.multiple_of(p * peer_rows, peer_rows), peer_rows), :]

    own_fwd = pltpu.make_async_copy(rows_of(fwd_out, me), rows_of(fwd_in, me), fwd_recv.at[planes - 1])
    own_fwd.start()

    def ahead(turn):
        out = (turn * 0)
        for t, far in enumerate(ORDER[planes]):
            out = jnp.where(turn == t, far, out)
        return out

    for turn, far in enumerate(ORDER[planes]):
        to_ga = lax.rem(ga + (planes - far), planes)

        def send(k, _):
            to_dev = jnp.bitwise_xor(dev, k)
            pltpu.make_async_remote_copy(
                rows_of(fwd_out, to_ga * per_plane + to_dev), rows_of(fwd_in, me), fwd_send, fwd_recv.at[turn],
                device_id=(to_ga, to_dev), device_id_type=MESH).start()
            return 0
        lax.fori_loop(0 if far else 1, per_plane, send, 0)

    lax.fori_loop(0, planes * levels // 2, slopes, 0, unroll=4)

    def row(b, i, z):
        return jnp.broadcast_to(coef[b, i, pl.ds(z, 1), :], (ROWS, LANES))

    def sweep(b, even, odd, store):
        def strip(ref, z, k):
            at = pl.ds(z * cells + ROWS * k, ROWS)
            return ref[at, :] if ref is half_way else ref[b, at, :]

        def advected(z):
            g = [strip(even, z, k) for k in range(groups)]
            if odd is not None:
                rate = row(b, 0, z)
                return [g[k] - rate * strip(odd, z, k) for k in range(groups)]
            east_c, west_c = row(b, 1, z), row(b, 2, z)
            east, west = neighbours_of(g)
            return [g[k] + (east_c * east[k] + west_c * west[k]) for k in range(groups)]

        def mix(z, below, here, above):
            mz, kz = row(b, 3, z), row(b, 4, z)
            store(z, [kz * here[k] + mz * (above[k] + below[k]) for k in range(groups)])

        def body(z, carry):
            below, here = carry
            above = advected(z + 1)
            mix(z, below, here, above)
            return here, above

        edge = advected(0)
        below, here = lax.fori_loop(0, levels - 1, body, (edge, edge), unroll=19)
        mix(levels - 1, below, here, here)

    def block(turn, _):
        b = lax.rem(ga + ahead(turn), planes)
        here_rows = pl.ds(pl.multiple_of(b * LANES, LANES), LANES)
        arrived = fwd_in.at[:, here_rows, :]
        pltpu.make_async_copy(arrived, arrived, fwd_recv.at[turn]).wait()
        wind = jnp.transpose(fwd_in[0, here_rows, :], (1, 0))
        heat_wet = jnp.transpose(fwd_in[1, here_rows, :], (1, 0))
        heat, wet = heat_wet[:zp], heat_wet[zp:]
        slope = (0.15 / keep_x) * jnp.tanh(wind[:zp])
        m = 0.1 + 0.15 * jax.nn.sigmoid(wind[zp:])
        keep = 1.0 - 2.0 * m
        for i, rows in enumerate((slope, side - slope, side + slope, keep_x * m, keep_x * keep)):
            coef[b, i] = rows
        flag = cloudy_ref[here_rows].astype(F32).reshape(1, LANES)
        dry = jnp.broadcast_to((0.5 * DRYING) * flag, (ROWS, LANES))
        mean_p, mean_c = total_of(0, b), total_of(1, b)
        aim_p = (wet - 0.5 * heat) - 0.5
        aim_c = heat + LATENT_HEAT * wet
        row_p = row_c = condensed = None

        for step in range(SUB):
            first = step == 0
            mean_p = mixed(mean_p, m, keep, levels)
            mean_c = mixed(mean_c, m, keep, levels)
            relax_p = RELAX_RATE * (aim_p - mean_p)
            relax_c = RELAX_RATE * (aim_c - mean_c)
            row_p = relax_p if first else mixed(row_p, m, keep, levels) + relax_p
            row_c = relax_c if first else mixed(row_c, m, keep, levels) + relax_c
            coef[b, 5] = row_p

            def cloud(z, mixed_cells):
                offset = row(b, 5, z)
                total = None
                for k in range(groups):
                    e = jnp.maximum(mixed_cells[k] + offset, 0.0)
                    total = e if total is None else total + e
                    at = pl.ds(z * cells + ROWS * k, ROWS)
                    if first:
                        half_way[at, :] = mixed_cells[k] - dry * e
                    else:
                        odd_p[b, at, :] = mixed_cells[k] - dry * e
                sums[0, b, pl.ds(z * ROWS, ROWS), :] = total

            if first:
                sweep(b, even_p, odd_p, cloud)
            else:
                sweep(b, half_way, None, cloud)
            excess = (0.5 * flag) * total_of(0, b)
            mean_p = mean_p + relax_p - DRYING * excess
            mean_c = mean_c + relax_c
            condensed = excess if condensed is None else condensed + excess

        coef[b, 5] = (row_p + (0.5 + 0.5 * row_c)) * (1.0 / DRYING)
        coef[b, 6] = row_c
        mean_w = (mean_p + (0.5 + 0.5 * mean_c)) * (1.0 / DRYING)
        mean_t = mean_c - LATENT_HEAT * mean_w

        ret_out[0, here_rows, :] = jnp.transpose(jnp.concatenate([mean_t, mean_w], axis=0), (1, 0))
        ret_out[1, here_rows, :] = jnp.transpose(jnp.concatenate([condensed, condensed], axis=0), (1, 0))

        def answer(k, _):
            to_dev = jnp.bitwise_xor(dev, k)
            pltpu.make_async_remote_copy(
                rows_of(ret_out, b * per_plane + to_dev), rows_of(ret_in, me), ret_send, ret_recv,
                device_id=(b, to_dev), device_id_type=MESH).start()
            return 0
        lax.fori_loop(jnp.where(turn == planes - 1, 1, 0), per_plane, answer, 0)

        @pl.when(turn == planes - 1)
        def _():
            pltpu.make_async_copy(rows_of(ret_out, me), rows_of(ret_in, me), ret_recv).start()

        return 0
    lax.fori_loop(0, planes, block, 0)

    def finish(b, _):
        def keep_cells(z, mixed_cells):
            for k in range(groups):
                half_way[pl.ds(z * cells + ROWS * k, ROWS), :] = mixed_cells[k]

        def combine(z, mixed_cells):
            add_w, add_c = row(b, 5, z), row(b, 6, z)
            for k in range(groups):
                gap = odd_p[b, pl.ds(z * cells + ROWS * k, ROWS), :]
                w = (gap + 0.5 * mixed_cells[k]) * (1.0 / DRYING) + add_w
                at = pl.ds(z * cells + k, ROWS, stride=groups)
                even_p[b, at, :] = w
                odd_c[b, at, :] = (mixed_cells[k] + add_c) - LATENT_HEAT * w

        sweep(b, even_c, odd_c, keep_cells)
        sweep(b, half_way, None, combine)
        lanes = pl.ds(pl.multiple_of(b * LANES, LANES), LANES)

        def narrow(z, _):
            at = pl.ds(z * cells, cells)
            theta_out[z, :, lanes] = odd_c[b, at, :].astype(theta_out.dtype)
            water_out[z, :, lanes] = even_p[b, at, :].astype(water_out.dtype)
            return 0
        return lax.fori_loop(0, levels, narrow, 0, unroll=29)
    lax.fori_loop(0, planes, finish, 0)
    state_out[...] = state[...]

    pltpu.make_async_copy(ret_in, ret_in, ret_recv).wait()
    back = [dot(ret_in[h], place[...], 0, 0) for h in range(2)]
    after = {2: back[0][:zp], 3: back[0][zp:], 4: back[1][:zp]}
    for f, value in after.items():
        old = state[f, :zp, :]
        new = old + STEP_WEIGHT * (value - old)
        state_out[f, :zp, :] = jnp.where(iota((zp, columns), 0) < levels, new, old)

    others = pl.ds(peer_rows, columns - peer_rows)
    for ref, sem in ((fwd_out, fwd_send), (ret_out, ret_send)):
        gone = ref.at[:, others, :]
        pltpu.make_async_copy(gone, gone, sem).wait()


def store_kernel(*refs):
    sems = refs[6]
    copies = [pltpu.make_async_copy(refs[i], refs[3 + i], sems.at[i]) for i in range(3)]
    for c in copies:
        c.start()
    for c in copies:
        c.wait()


def on_device(planes, per_plane, column_state, neighbours, crm_slot, cloudy, crm_theta, crm_water):
    fields, lev, columns = column_state.shape
    levels, cells, _ = crm_theta.shape
    zp = -(-levels // ROWS) * ROWS
    elements = columns // 4
    blocks = columns // LANES
    wide = pltpu.VMEM((2, columns, 2 * zp), F32)
    halo = pltpu.VMEM((fields * lev, elements), F32)
    narrow_block = pltpu.VMEM((blocks, levels, cells, LANES), crm_theta.dtype)
    wide_block = pltpu.VMEM((blocks, levels * cells, LANES), F32)
    dma = pltpu.SemaphoreType.DMA
    hbm, vmem = pl.BlockSpec(memory_space=pl.ANY), pl.BlockSpec(memory_space=pltpu.VMEM)
    inputs = [pltpu.with_memory_space_constraint(a, pltpu.HBM)
              for a in (column_state, neighbours.T, crm_slot, cloudy, crm_theta, crm_water)]
    results = pl.pallas_call(
        functools.partial(step_kernel, (planes, per_plane, levels, cells)),
        out_shape=tuple(jax.ShapeDtypeStruct(a.shape, a.dtype) for a in (column_state, crm_theta, crm_water)),
        in_specs=[hbm] * 6,
        out_specs=(vmem, vmem, vmem),
        scratch_shapes=[
            pltpu.VMEM((4, elements), jnp.int32), pltpu.VMEM((columns,), jnp.int32), pltpu.VMEM((columns,), jnp.int32),
            pltpu.VMEM(column_state.shape, F32), halo, halo, halo, pltpu.VMEM((columns, columns), BF16),
            narrow_block, narrow_block, wide_block, wide_block, wide_block, wide_block,
            pltpu.VMEM((levels * cells, LANES), F32),
            pltpu.VMEM((blocks, 7, zp, LANES), F32), pltpu.VMEM((2, blocks, zp * ROWS, LANES), F32),
            wide, wide, wide, wide,
            dma((4 + 2 * blocks,)), dma((2,)), dma((2,)), dma, dma((planes,)), dma, dma,
        ],
        compiler_params=pltpu.CompilerParams(collective_id=0, has_side_effects=True, vmem_limit_bytes=36 * 2 ** 20),
        name="physics_step",
    )(*inputs)
    return pl.pallas_call(
        store_kernel,
        out_shape=tuple(jax.ShapeDtypeStruct(a.shape, a.dtype) for a in results),
        in_specs=[vmem] * 3,
        out_specs=(hbm, hbm, hbm),
        scratch_shapes=[dma((3,))],
        compiler_params=pltpu.CompilerParams(vmem_limit_bytes=16 * 2 ** 20),
        name="store",
    )(*results)


def solution(mesh):
    split = ("ga", "dev")
    planes, per_plane = mesh.shape["ga"], mesh.shape["dev"]
    return jax.shard_map(
        functools.partial(on_device, planes, per_plane),
        mesh=mesh,
        in_specs=(P(None, None, split), P(split, None), P(split), P(split), P(None, None, split), P(None, None, split)),
        out_specs=(P(None, None, split), P(None, None, split), P(None, None, split)),
        check_vma=False,
    )
```

```python
import functools

import jax
import jax.numpy as jnp
from jax import lax
from jax.experimental import pallas as pl
from jax.experimental.pallas import tpu as pltpu
from jax.sharding import PartitionSpec as P

SUB = 2
DIFFUSION = 0.15
X_DIFFUSION = 0.2
RELAX_RATE = 0.2
LATENT_HEAT = 0.8
DRYING = 1.0 + 0.5 * LATENT_HEAT
STEP_WEIGHT = 0.5
LANES = 128
ORDER = {4: (2, 1, 3, 0)}
SERVED = {4: (2, 1, 3, 0)}
ROWS = 8
MESH = pl.DeviceIdType.MESH
F32, BF16 = jnp.float32, jnp.bfloat16


def pieces(x):
    high = x.astype(BF16)
    return high, (x - high.astype(F32)).astype(BF16)


def dot(a, b, left=1, right=0):
    dims = (((left,), (right,)), ((), ()))
    one = functools.partial(lax.dot_general, dimension_numbers=dims, preferred_element_type=F32)
    if a.dtype == BF16:
        parts = [one(a, p) for p in pieces(b)]
    else:
        parts = [one(p, b) for p in pieces(a)]
    return parts[1] + parts[0]


def iota(shape, dim):
    return lax.broadcasted_iota(jnp.int32, shape, dim)


def ones_where(mask, value=1.0):
    return jnp.where(mask, value, 0.0).astype(BF16)


def neighbours_of(g):
    east = g[1:] + [pltpu.roll(g[0], ROWS - 1, 0)]
    west = [pltpu.roll(g[-1], 1, 0)] + g[:-1]
    return east, west


def mixed(rows, m, keep, levels):
    up = pltpu.roll(rows, rows.shape[0] - 1, 0)
    down = pltpu.roll(rows, 1, 0)
    z = iota(rows.shape, 0)
    up = jnp.where(z == levels - 1, rows, up)
    down = jnp.where(z == 0, rows, down)
    return keep * rows + m * (up + down)


def step_kernel(sizes, state_hbm, nb_hbm, slot_hbm, cloudy_hbm, theta_hbm, water_hbm,
                state_out, theta_out, water_out,
                nb_ref, slot_ref, cloudy_ref, state, mean, low, high, place, theta_in, water_in, even_p, odd_p, even_c, odd_c, half_way, coef, sums,
                pack, start_out, start_in, fwd_out, fwd_in, ret_out, ret_in,
                load_sem, halo_send, halo_recv, start_send, start_recv, fwd_send, fwd_recv, ret_send, ret_recv):
    planes, per_plane, levels, cells = sizes
    devices = planes * per_plane
    fields, lev, columns = state.shape
    elements = columns // 4
    peer_rows = columns // devices
    zp = coef.shape[2]
    groups = cells // ROWS
    ga, dev = lax.axis_index("ga"), lax.axis_index("dev")
    me = ga * per_plane + dev
    keep_x = 1.0 - 2.0 * X_DIFFUSION
    side = X_DIFFUSION / keep_x

    load_state = pltpu.make_async_copy(state_hbm, state, load_sem.at[0])
    load_state.start()
    small = [pltpu.make_async_copy(src, dst, load_sem.at[1 + 2 * planes + i]) for i, (src, dst) in enumerate(
        ((nb_hbm, nb_ref), (slot_hbm, slot_ref), (cloudy_hbm, cloudy_ref)))]
    for c in small:
        c.start()
    loads = []
    for b in range(planes):
        for j, (src, dst) in enumerate(((theta_hbm, theta_in), (water_hbm, water_in))):
            loads.append(pltpu.make_async_copy(
                src.at[:, :, pl.ds(b * LANES, LANES)], dst.at[b], load_sem.at[1 + 2 * b + j]))
            loads[-1].start()

    barrier = pltpu.get_barrier_semaphore()

    for far in ORDER[planes]:
        to_ga = lax.rem(ga + far, planes)

        def greet(k, _):
            pl.semaphore_signal(barrier, inc=1, device_id=(to_ga, jnp.bitwise_xor(dev, k)), device_id_type=MESH)
            return 0
        lax.fori_loop(0 if far else 1, per_plane, greet, 0)

    load_state.wait()
    flat = state[...].reshape(fields * lev, columns)
    gather = ones_where(iota((columns, elements), 0) // 4 == iota((columns, elements), 1), 0.25)
    mean[...] = dot(flat, gather)
    pl.semaphore_wait(barrier, devices - 1)

    halo = []
    for j, (shift, dst) in enumerate(((1, low), (devices - 1, high))):
        p = lax.rem(me + shift, devices)
        halo.append(pltpu.make_async_remote_copy(
            mean, dst, halo_send.at[j], halo_recv.at[j],
            device_id=(p // per_plane, lax.rem(p, per_plane)), device_id_type=MESH))
        halo[-1].start()

    for c in small:
        c.wait()
    def rows_of(ref, p, count):
        return ref.at[:, pl.ds(pl.multiple_of(p * count, count), count), :]

    def send_all(src, dst, sent, got, count):
        for far in ORDER[planes]:
            to_ga = lax.rem(ga + (planes - far), planes)

            def send(k, _):
                to_dev = jnp.bitwise_xor(dev, k)
                pltpu.make_async_remote_copy(
                    rows_of(src, to_ga * per_plane + to_dev, count), rows_of(dst, me, count), sent, got(far),
                    device_id=(to_ga, to_dev), device_id_type=MESH).start()
                return 0
            lax.fori_loop(0 if far else 1, per_plane, send, 0)

    relative = jnp.bitwise_and(nb_ref[...] - me * elements + elements, elements * devices - 1)

    def counts(part):
        total = None
        for k in range(4):
            hit = jnp.where(relative[k:k + 1] - part * elements == iota((elements, elements), 0), 1.0, 0.0)
            total = hit if total is None else total + hit
        return total.astype(BF16)

    slot = slot_ref[...].reshape(1, columns)
    dest_row = slot // columns * peer_rows + lax.rem(slot, peer_rows)
    place[...] = ones_where(iota((columns, columns), 0) == dest_row)
    own = mean[...]
    laplace = dot(own, counts(1)) - 4.0 * own
    inv = 1.0 / cells
    for c in loads:
        c.wait()

    def widen(i, _):
        b, pair = i // (levels // 2), lax.rem(i, levels // 2)
        for j in range(2):
            z = 2 * pair + j
            warmth, wetness = theta_in[b, z].astype(F32), water_in[b, z].astype(F32)
            gap = (wetness - 0.5 * warmth) - 0.5
            for part, (dst, g) in enumerate(((even_p, gap), (even_c, warmth + LATENT_HEAT * wetness))):
                dst[b, pl.ds(z * cells, cells), :] = g
                sums[part, b, pl.ds(z * ROWS, ROWS), :] = functools.reduce(
                    jnp.add, [g[ROWS * k:ROWS * k + ROWS] for k in range(groups)])
        return 0
    lax.fori_loop(0, planes * levels // 2, widen, 0, unroll=4)

    def slopes(i, _):
        b, pair = i // (levels // 2), lax.rem(i, levels // 2)
        for j in range(2):
            z = 2 * pair + j
            for even, odd in ((even_p, odd_p), (even_c, odd_c)):
                g = [even[b, pl.ds(z * cells + k, ROWS, stride=groups), :] for k in range(groups)]
                east, west = neighbours_of(g)
                for k in range(groups):
                    at = pl.ds(z * cells + ROWS * k, ROWS)
                    even[b, at, :] = g[k] + side * (east[k] + west[k])
                    odd[b, at, :] = east[k] - west[k]
        return 0

    def total_of(part, b):
        rows = [sums[part, b, pl.ds(k, zp, stride=ROWS), :] for k in range(ROWS)]
        return functools.reduce(jnp.add, rows) * inv

    for b in range(planes):
        total = total_of(1, b)
        pack[...] = jnp.transpose(jnp.concatenate([total, total], axis=0), (1, 0))
        evens, odds = pack[pl.ds(0, LANES // 2, stride=2), :], pack[pl.ds(1, LANES // 2, stride=2), :]
        start_out[0, pl.ds(b * (LANES // 2), LANES // 2), :] = jnp.where(iota(evens.shape, 1) < zp, evens, odds)
    halo[0].wait()
    halo[1].wait()
    laplace = laplace + (dot(low[...], counts(0)) + dot(high[...], counts(2)))
    spread = ones_where(iota((elements, columns), 0) == iota((elements, columns), 1) // 4)
    flat = flat + DIFFUSION * dot(laplace, spread)
    state[...] = flat.reshape(fields, lev, columns)

    kept = [flat[f * lev:f * lev + zp] for f in range(fields)]
    sent = (kept[0], kept[1]), (kept[2], kept[3] + kept[4] + kept[5])
    for h in range(2):
        fwd_out[h] = dot(place[...], jnp.concatenate(sent[h], axis=0), 1, 1)

    own_fwd = pltpu.make_async_copy(rows_of(fwd_out, me, peer_rows), rows_of(fwd_in, me, peer_rows), fwd_recv.at[0])
    own_fwd.start()

    def ahead(turn):
        out = turn * 0
        for t, far in enumerate(SERVED[planes]):
            out = jnp.where(turn == t, far, out)
        return out

    send_all(fwd_out, fwd_in, fwd_send, lambda far: fwd_recv.at[far], peer_rows)

    lax.fori_loop(0, planes * levels // 2, slopes, 0, unroll=4)
    own_start = pltpu.make_async_copy(
        rows_of(start_out, me, peer_rows // 2), rows_of(start_in, me, peer_rows // 2), start_recv)
    own_start.start()
    send_all(start_out, start_in, start_send, lambda far: start_recv, peer_rows // 2)


    def row(b, i, z):
        return jnp.broadcast_to(coef[b, i, pl.ds(z, 1), :], (ROWS, LANES))

    def sweep(b, even, odd, store):
        def strip(ref, z, k):
            at = pl.ds(z * cells + ROWS * k, ROWS)
            return ref[at, :] if ref is half_way else ref[b, at, :]

        def advected(z):
            g = [strip(even, z, k) for k in range(groups)]
            if odd is not None:
                rate = row(b, 0, z)
                return [g[k] - rate * strip(odd, z, k) for k in range(groups)]
            east_c, west_c = row(b, 1, z), row(b, 2, z)
            east, west = neighbours_of(g)
            return [g[k] + (east_c * east[k] + west_c * west[k]) for k in range(groups)]

        def mix(z, below, here, above):
            mz, kz = row(b, 3, z), row(b, 4, z)
            store(z, [kz * here[k] + mz * (above[k] + below[k]) for k in range(groups)])

        def body(z, carry):
            below, here = carry
            above = advected(z + 1)
            mix(z, below, here, above)
            return here, above

        edge = advected(0)
        below, here = lax.fori_loop(0, levels - 1, body, (edge, edge), unroll=19)
        mix(levels - 1, below, here, here)

    def block(turn, _):
        far = ahead(turn)
        b = lax.rem(ga + far, planes)
        here_rows = pl.ds(pl.multiple_of(b * LANES, LANES), LANES)
        arrived = fwd_in.at[:, here_rows, :]
        pltpu.make_async_copy(arrived, arrived, fwd_recv.at[far]).wait()
        wind = jnp.transpose(fwd_in[0, here_rows, :], (1, 0))
        heat_wet = jnp.transpose(fwd_in[1, here_rows, :], (1, 0))
        heat, wet = heat_wet[:zp], heat_wet[zp:]
        slope = (0.15 / keep_x) * jnp.tanh(wind[:zp])
        m = 0.1 + 0.15 * jax.nn.sigmoid(wind[zp:])
        keep = 1.0 - 2.0 * m
        for i, rows in enumerate((slope, side - slope, side + slope, keep_x * m, keep_x * keep)):
            coef[b, i] = rows
        flag = cloudy_ref[here_rows].astype(F32).reshape(1, LANES)
        dry = jnp.broadcast_to((0.5 * DRYING) * flag, (ROWS, LANES))
        mean_p = total_of(0, b)
        aim_p = (wet - 0.5 * heat) - 0.5
        coef[b, 6] = heat + LATENT_HEAT * wet
        row_p = condensed = None

        for step in range(SUB):
            first = step == 0
            mean_p = mixed(mean_p, m, keep, levels)
            relax_p = RELAX_RATE * (aim_p - mean_p)
            row_p = relax_p if first else mixed(row_p, m, keep, levels) + relax_p
            coef[b, 5] = row_p

            def cloud(z, mixed_cells):
                offset = row(b, 5, z)
                total = None
                for k in range(groups):
                    e = jnp.maximum(mixed_cells[k] + offset, 0.0)
                    total = e if total is None else total + e
                    at = pl.ds(z * cells + ROWS * k, ROWS)
                    if first:
                        half_way[at, :] = mixed_cells[k] - dry * e
                    else:
                        odd_p[b, at, :] = mixed_cells[k] - dry * e
                sums[0, b, pl.ds(z * ROWS, ROWS), :] = total

            if first:
                sweep(b, even_p, odd_p, cloud)
            else:
                sweep(b, half_way, None, cloud)
            excess = (0.5 * flag) * total_of(0, b)
            mean_p = mean_p + relax_p - DRYING * excess
            condensed = excess if condensed is None else condensed + excess

        ret_out[0, here_rows, :] = jnp.transpose(jnp.concatenate([mean_p, condensed], axis=0), (1, 0))

        def answer(k, _):
            to_dev = jnp.bitwise_xor(dev, k)
            pltpu.make_async_remote_copy(
                rows_of(ret_out, b * per_plane + to_dev, peer_rows), rows_of(ret_in, me, peer_rows), ret_send, ret_recv,
                device_id=(b, to_dev), device_id_type=MESH).start()
            return 0
        lax.fori_loop(jnp.where(far == 0, 1, 0), per_plane, answer, 0)

        @pl.when(far == 0)
        def _():
            pltpu.make_async_copy(rows_of(ret_out, me, peer_rows), rows_of(ret_in, me, peer_rows), ret_recv).start()

        return 0
    lax.fori_loop(0, planes, block, 0)

    def relaxed(mean, aim, m, keep):
        added = None
        for step in range(SUB):
            mean = mixed(mean, m, keep, levels)
            pull = RELAX_RATE * (aim - mean)
            added = pull if added is None else mixed(added, m, keep, levels) + pull
            mean = mean + pull
        return mean, added

    def finish(b, _):
        _, row_c = relaxed(total_of(1, b), coef[b, 6], coef[b, 3] * (1.0 / keep_x), coef[b, 4] * (1.0 / keep_x))
        coef[b, 5] = (coef[b, 5] + (0.5 + 0.5 * row_c)) * (1.0 / DRYING)
        coef[b, 6] = row_c

        def keep_cells(z, mixed_cells):
            for k in range(groups):
                half_way[pl.ds(z * cells + ROWS * k, ROWS), :] = mixed_cells[k]

        def combine(z, mixed_cells):
            add_w, add_c = row(b, 5, z), row(b, 6, z)
            for k in range(groups):
                gap = odd_p[b, pl.ds(z * cells + ROWS * k, ROWS), :]
                w = (gap + 0.5 * mixed_cells[k]) * (1.0 / DRYING) + add_w
                at = pl.ds(z * cells + k, ROWS, stride=groups)
                even_p[b, at, :] = w
                odd_c[b, at, :] = (mixed_cells[k] + add_c) - LATENT_HEAT * w

        sweep(b, even_c, odd_c, keep_cells)
        sweep(b, half_way, None, combine)
        lanes = pl.ds(pl.multiple_of(b * LANES, LANES), LANES)

        def narrow(z, _):
            at = pl.ds(z * cells, cells)
            theta_out[z, :, lanes] = odd_c[b, at, :].astype(theta_out.dtype)
            water_out[z, :, lanes] = even_p[b, at, :].astype(water_out.dtype)
            return 0
        return lax.fori_loop(0, levels, narrow, 0, unroll=29)
    lax.fori_loop(0, planes, finish, 0)
    state_out[...] = state[...]

    pltpu.make_async_copy(start_in, start_in, start_recv).wait()
    source = 2 * iota((columns // 2, columns), 0)
    first_c = (dot(start_in[0], ones_where(source == dest_row), 0, 0)[:zp]
               + dot(start_in[0], ones_where(source + 1 == dest_row), 0, 0)[zp:])
    column_m = 0.1 + 0.15 * jax.nn.sigmoid(state[1, :zp, :])
    column_wet = (state[3, :zp, :] + state[4, :zp, :]) + state[5, :zp, :]
    mean_c, _ = relaxed(first_c, state[2, :zp, :] + LATENT_HEAT * column_wet, column_m, 1.0 - 2.0 * column_m)

    pltpu.make_async_copy(ret_in, ret_in, ret_recv).wait()
    back = dot(ret_in[0], place[...], 0, 0)
    mean_w = (back[:zp] + (0.5 + 0.5 * mean_c)) * (1.0 / DRYING)
    after = {2: mean_c - LATENT_HEAT * mean_w, 3: mean_w, 4: back[zp:]}
    for f, value in after.items():
        old = state[f, :zp, :]
        new = old + STEP_WEIGHT * (value - old)
        state_out[f, :zp, :] = jnp.where(iota((zp, columns), 0) < levels, new, old)

    for ref, sem, count in ((start_out, start_send, peer_rows // 2), (fwd_out, fwd_send, peer_rows), (ret_out, ret_send, peer_rows)):
        gone = ref.at[:, pl.ds(count, (devices - 1) * count), :]
        pltpu.make_async_copy(gone, gone, sem).wait()


def store_kernel(*refs):
    sems = refs[6]
    copies = [pltpu.make_async_copy(refs[i], refs[3 + i], sems.at[i]) for i in range(3)]
    for c in copies:
        c.start()
    for c in copies:
        c.wait()


def on_device(planes, per_plane, column_state, neighbours, crm_slot, cloudy, crm_theta, crm_water):
    fields, lev, columns = column_state.shape
    levels, cells, _ = crm_theta.shape
    zp = -(-levels // ROWS) * ROWS
    elements = columns // 4
    blocks = columns // LANES
    wide, answer = (pltpu.VMEM((n, columns, 2 * zp), F32) for n in (2, 1))
    start = pltpu.VMEM((1, columns // 2, 2 * zp), F32)
    halo = pltpu.VMEM((fields * lev, elements), F32)
    narrow_block = pltpu.VMEM((blocks, levels, cells, LANES), crm_theta.dtype)
    wide_block = pltpu.VMEM((blocks, levels * cells, LANES), F32)
    dma = pltpu.SemaphoreType.DMA
    hbm, vmem = pl.BlockSpec(memory_space=pl.ANY), pl.BlockSpec(memory_space=pltpu.VMEM)
    inputs = [pltpu.with_memory_space_constraint(a, pltpu.HBM)
              for a in (column_state, neighbours.T, crm_slot, cloudy, crm_theta, crm_water)]
    results = pl.pallas_call(
        functools.partial(step_kernel, (planes, per_plane, levels, cells)),
        out_shape=tuple(jax.ShapeDtypeStruct(a.shape, a.dtype) for a in (column_state, crm_theta, crm_water)),
        in_specs=[hbm] * 6,
        out_specs=(vmem, vmem, vmem),
        scratch_shapes=[
            pltpu.VMEM((4, elements), jnp.int32), pltpu.VMEM((columns,), jnp.int32), pltpu.VMEM((columns,), jnp.int32),
            pltpu.VMEM(column_state.shape, F32), halo, halo, halo, pltpu.VMEM((columns, columns), BF16),
            narrow_block, narrow_block, wide_block, wide_block, wide_block, wide_block,
            pltpu.VMEM((levels * cells, LANES), F32),
            pltpu.VMEM((blocks, 7, zp, LANES), F32), pltpu.VMEM((2, blocks, zp * ROWS, LANES), F32),
            pltpu.VMEM((LANES, LANES), F32), start, start, wide, wide, answer, answer,
            dma((4 + 2 * blocks,)), dma((2,)), dma((2,)), dma, dma, dma, dma((planes,)), dma, dma,
        ],
        compiler_params=pltpu.CompilerParams(collective_id=0, has_side_effects=True, vmem_limit_bytes=36 * 2 ** 20),
        name="physics_step",
    )(*inputs)
    return pl.pallas_call(
        store_kernel,
        out_shape=tuple(jax.ShapeDtypeStruct(a.shape, a.dtype) for a in results),
        in_specs=[vmem] * 3,
        out_specs=(hbm, hbm, hbm),
        scratch_shapes=[dma((3,))],
        compiler_params=pltpu.CompilerParams(vmem_limit_bytes=16 * 2 ** 20),
        name="store",
    )(*results)


def solution(mesh):
    split = ("ga", "dev")
    planes, per_plane = mesh.shape["ga"], mesh.shape["dev"]
    return jax.shard_map(
        functools.partial(on_device, planes, per_plane),
        mesh=mesh,
        in_specs=(P(None, None, split), P(split, None), P(split), P(split), P(None, None, split), P(None, None, split)),
        out_specs=(P(None, None, split), P(None, None, split), P(None, None, split)),
        check_vma=False,
    )
```

```python
import functools

import jax
import jax.numpy as jnp
from jax import lax
from jax.experimental import pallas as pl
from jax.experimental.pallas import tpu as pltpu
from jax.sharding import PartitionSpec as P

SUB = 2
DIFFUSION = 0.15
X_DIFFUSION = 0.2
RELAX_RATE = 0.2
LATENT_HEAT = 0.8
DRYING = 1.0 + 0.5 * LATENT_HEAT
STEP_WEIGHT = 0.5
LANES = 128
ORDER = {4: (2, 1, 3, 0)}
SERVED = {4: (2, 1, 3, 0)}
ROWS = 8
MESH = pl.DeviceIdType.MESH
F32, BF16 = jnp.float32, jnp.bfloat16


def pieces(x):
    high = x.astype(BF16)
    return high, (x - high.astype(F32)).astype(BF16)


def dot(a, b, left=1, right=0):
    dims = (((left,), (right,)), ((), ()))
    one = functools.partial(lax.dot_general, dimension_numbers=dims, preferred_element_type=F32)
    if a.dtype == BF16:
        parts = [one(a, p) for p in pieces(b)]
    else:
        parts = [one(p, b) for p in pieces(a)]
    return parts[1] + parts[0]


def iota(shape, dim):
    return lax.broadcasted_iota(jnp.int32, shape, dim)


def ones_where(mask, value=1.0):
    return jnp.where(mask, value, 0.0).astype(BF16)


def neighbours_of(g):
    east = g[1:] + [pltpu.roll(g[0], ROWS - 1, 0)]
    west = [pltpu.roll(g[-1], 1, 0)] + g[:-1]
    return east, west


def mixed(rows, m, keep, levels):
    up = pltpu.roll(rows, rows.shape[0] - 1, 0)
    down = pltpu.roll(rows, 1, 0)
    z = iota(rows.shape, 0)
    up = jnp.where(z == levels - 1, rows, up)
    down = jnp.where(z == 0, rows, down)
    return keep * rows + m * (up + down)


def step_kernel(sizes, state_hbm, nb_hbm, slot_hbm, cloudy_hbm, theta_hbm, water_hbm,
                state_out, theta_out, water_out,
                nb_ref, slot_ref, cloudy_ref, state, mean, low, high, rest_mean, rest_low, rest_high, place, theta_in, water_in, even_p, odd_p, even_c, odd_c, half_way, coef, sums,
                pack, start_out, start_in, fwd_out, fwd_in, ret_out, ret_in,
                load_sem, halo_send, halo_recv, start_send, start_recv, fwd_send, fwd_recv, ret_send, ret_recv):
    planes, per_plane, levels, cells = sizes
    devices = planes * per_plane
    fields, lev, columns = state.shape
    elements = columns // 4
    peer_rows = columns // devices
    zp = coef.shape[2]
    groups = cells // ROWS
    ga, dev = lax.axis_index("ga"), lax.axis_index("dev")
    me = ga * per_plane + dev
    keep_x = 1.0 - 2.0 * X_DIFFUSION
    side = X_DIFFUSION / keep_x

    load_state = pltpu.make_async_copy(state_hbm, state, load_sem.at[0])
    load_state.start()
    small = [pltpu.make_async_copy(src, dst, load_sem.at[1 + 2 * planes + i]) for i, (src, dst) in enumerate(
        ((nb_hbm, nb_ref), (slot_hbm, slot_ref), (cloudy_hbm, cloudy_ref)))]
    for c in small:
        c.start()
    loads = []
    for b in range(planes):
        for j, (src, dst) in enumerate(((theta_hbm, theta_in), (water_hbm, water_in))):
            loads.append(pltpu.make_async_copy(
                src.at[:, :, pl.ds(b * LANES, LANES)], dst.at[b], load_sem.at[1 + 2 * b + j]))
            loads[-1].start()

    barrier = pltpu.get_barrier_semaphore()

    for far in ORDER[planes]:
        to_ga = lax.rem(ga + far, planes)

        def greet(k, _):
            pl.semaphore_signal(barrier, inc=1, device_id=(to_ga, jnp.bitwise_xor(dev, k)), device_id_type=MESH)
            return 0
        lax.fori_loop(0 if far else 1, per_plane, greet, 0)

    load_state.wait()
    gather = ones_where(iota((columns, elements), 0) // 4 == iota((columns, elements), 1), 0.25)

    def leading():
        total = (state[3, :zp, :] + state[4, :zp, :]) + state[5, :zp, :]
        return jnp.concatenate([state[f, :zp, :] for f in range(3)] + [total], axis=0)

    def trailing():
        return jnp.concatenate([state[f, zp:, :] for f in range(3)] + [state[f] for f in range(3, fields)], axis=0)
    mean[...] = dot(leading(), gather)
    pl.semaphore_wait(barrier, devices - 1)

    def exchange(src, sinks, first):
        copies = []
        for j, (shift, dst) in enumerate(zip((1, devices - 1), sinks)):
            p = lax.rem(me + shift, devices)
            copies.append(pltpu.make_async_remote_copy(
                src, dst, halo_send.at[first + j], halo_recv.at[first + j],
                device_id=(p // per_plane, lax.rem(p, per_plane)), device_id_type=MESH))
            copies[-1].start()
        return copies
    halo = exchange(mean, (low, high), 0)
    rest_mean[...] = dot(trailing(), gather)
    rest_halo = exchange(rest_mean, (rest_low, rest_high), 2)
    for c in small:
        c.wait()

    def rows_of(ref, p, count):
        return ref.at[:, pl.ds(pl.multiple_of(p * count, count), count), :]

    def send_all(src, dst, sent, got, count):
        for far in ORDER[planes]:
            to_ga = lax.rem(ga + (planes - far), planes)

            def send(k, _):
                to_dev = jnp.bitwise_xor(dev, k)
                pltpu.make_async_remote_copy(
                    rows_of(src, to_ga * per_plane + to_dev, count), rows_of(dst, me, count), sent, got(far),
                    device_id=(to_ga, to_dev), device_id_type=MESH).start()
                return 0
            lax.fori_loop(0 if far else 1, per_plane, send, 0)

    relative = jnp.bitwise_and(nb_ref[...] - me * elements + elements, elements * devices - 1)

    def counts(part):
        total = None
        for k in range(4):
            hit = jnp.where(relative[k:k + 1] - part * elements == iota((elements, elements), 0), 1.0, 0.0)
            total = hit if total is None else total + hit
        return total.astype(BF16)

    slot = slot_ref[...].reshape(1, columns)
    dest_row = slot // columns * peer_rows + lax.rem(slot, peer_rows)
    place[...] = ones_where(iota((columns, columns), 0) == dest_row)
    weights = [counts(part) for part in range(3)]
    own = mean[...]
    laplace = dot(own, weights[1]) - 4.0 * own
    inv = 1.0 / cells
    for c in loads:
        c.wait()

    def widen(i, _):
        b, pair = i // (levels // 2), lax.rem(i, levels // 2)
        for j in range(2):
            z = 2 * pair + j
            warmth, wetness = theta_in[b, z].astype(F32), water_in[b, z].astype(F32)
            gap = (wetness - 0.5 * warmth) - 0.5
            for part, (dst, g) in enumerate(((even_p, gap), (even_c, warmth + LATENT_HEAT * wetness))):
                dst[b, pl.ds(z * cells, cells), :] = g
                sums[part, b, pl.ds(z * ROWS, ROWS), :] = functools.reduce(
                    jnp.add, [g[ROWS * k:ROWS * k + ROWS] for k in range(groups)])
        return 0
    lax.fori_loop(0, planes * levels // 2, widen, 0, unroll=4)

    def slopes(i, _):
        b, pair = i // (levels // 2), lax.rem(i, levels // 2)
        for j in range(2):
            z = 2 * pair + j
            for even, odd in ((even_p, odd_p), (even_c, odd_c)):
                g = [even[b, pl.ds(z * cells + k, ROWS, stride=groups), :] for k in range(groups)]
                east, west = neighbours_of(g)
                for k in range(groups):
                    at = pl.ds(z * cells + ROWS * k, ROWS)
                    even[b, at, :] = g[k] + side * (east[k] + west[k])
                    odd[b, at, :] = east[k] - west[k]
        return 0

    def total_of(part, b):
        rows = [sums[part, b, pl.ds(k, zp, stride=ROWS), :] for k in range(ROWS)]
        return functools.reduce(jnp.add, rows) * inv

    for b in range(planes):
        total = total_of(1, b)
        pack[...] = jnp.transpose(jnp.concatenate([total, total], axis=0), (1, 0))
        evens, odds = pack[pl.ds(0, LANES // 2, stride=2), :], pack[pl.ds(1, LANES // 2, stride=2), :]
        start_out[0, pl.ds(b * (LANES // 2), LANES // 2), :] = jnp.where(iota(evens.shape, 1) < zp, evens, odds)
    halo[0].wait()
    halo[1].wait()
    laplace = laplace + (dot(low[...], weights[0]) + dot(high[...], weights[2]))
    spread = ones_where(iota((elements, columns), 0) == iota((elements, columns), 1) // 4)
    lead = leading() + DIFFUSION * dot(laplace, spread)
    for h in range(2):
        fwd_out[h] = dot(place[...], lead[2 * zp * h:2 * zp * (h + 1)], 1, 1)

    own_fwd = pltpu.make_async_copy(rows_of(fwd_out, me, peer_rows), rows_of(fwd_in, me, peer_rows), fwd_recv.at[0])
    own_fwd.start()

    def ahead(turn):
        out = turn * 0
        for t, far in enumerate(SERVED[planes]):
            out = jnp.where(turn == t, far, out)
        return out

    send_all(fwd_out, fwd_in, fwd_send, lambda far: fwd_recv.at[far], peer_rows)
    state_rest = trailing()
    for f in range(3):
        state[f, :zp, :] = lead[f * zp:(f + 1) * zp]

    lax.fori_loop(0, planes * levels // 2, slopes, 0, unroll=4)
    own_start = pltpu.make_async_copy(
        rows_of(start_out, me, peer_rows // 2), rows_of(start_in, me, peer_rows // 2), start_recv)
    own_start.start()
    send_all(start_out, start_in, start_send, lambda far: start_recv, peer_rows // 2)


    rest_halo[0].wait()
    rest_halo[1].wait()
    own = rest_mean[...]
    laplace = (dot(own, weights[1]) - 4.0 * own) + (dot(rest_low[...], weights[0]) + dot(rest_high[...], weights[2]))
    state_rest = state_rest + DIFFUSION * dot(laplace, spread)
    tops = lev - zp
    for f in range(3):
        state[f, zp:, :] = state_rest[f * tops:(f + 1) * tops]
        state[3 + f] = state_rest[3 * tops + f * lev:3 * tops + (f + 1) * lev]

    def row(b, i, z):
        return jnp.broadcast_to(coef[b, i, pl.ds(z, 1), :], (ROWS, LANES))

    def sweep(b, even, odd, store):
        def strip(ref, z, k):
            at = pl.ds(z * cells + ROWS * k, ROWS)
            return ref[at, :] if ref is half_way else ref[b, at, :]

        def advected(z):
            g = [strip(even, z, k) for k in range(groups)]
            if odd is not None:
                rate = row(b, 0, z)
                return [g[k] - rate * strip(odd, z, k) for k in range(groups)]
            east_c, west_c = row(b, 1, z), row(b, 2, z)
            east, west = neighbours_of(g)
            return [g[k] + (east_c * east[k] + west_c * west[k]) for k in range(groups)]

        def mix(z, below, here, above):
            mz, kz = row(b, 3, z), row(b, 4, z)
            store(z, [kz * here[k] + mz * (above[k] + below[k]) for k in range(groups)])

        def body(z, carry):
            below, here = carry
            above = advected(z + 1)
            mix(z, below, here, above)
            return here, above

        edge = advected(0)
        below, here = lax.fori_loop(0, levels - 1, body, (edge, edge), unroll=19)
        mix(levels - 1, below, here, here)

    def block(turn, _):
        far = ahead(turn)
        b = lax.rem(ga + far, planes)
        here_rows = pl.ds(pl.multiple_of(b * LANES, LANES), LANES)
        arrived = fwd_in.at[:, here_rows, :]
        pltpu.make_async_copy(arrived, arrived, fwd_recv.at[far]).wait()
        wind = jnp.transpose(fwd_in[0, here_rows, :], (1, 0))
        heat_wet = jnp.transpose(fwd_in[1, here_rows, :], (1, 0))
        heat, wet = heat_wet[:zp], heat_wet[zp:]
        slope = (0.15 / keep_x) * jnp.tanh(wind[:zp])
        m = 0.1 + 0.15 * jax.nn.sigmoid(wind[zp:])
        keep = 1.0 - 2.0 * m
        for i, rows in enumerate((slope, side - slope, side + slope, keep_x * m, keep_x * keep)):
            coef[b, i] = rows
        flag = cloudy_ref[here_rows].astype(F32).reshape(1, LANES)
        dry = jnp.broadcast_to((0.5 * DRYING) * flag, (ROWS, LANES))
        mean_p = total_of(0, b)
        aim_p = (wet - 0.5 * heat) - 0.5
        coef[b, 6] = heat + LATENT_HEAT * wet
        row_p = condensed = None

        for step in range(SUB):
            first = step == 0
            mean_p = mixed(mean_p, m, keep, levels)
            relax_p = RELAX_RATE * (aim_p - mean_p)
            row_p = relax_p if first else mixed(row_p, m, keep, levels) + relax_p
            coef[b, 5] = row_p

            def cloud(z, mixed_cells):
                offset = row(b, 5, z)
                total = None
                for k in range(groups):
                    e = jnp.maximum(mixed_cells[k] + offset, 0.0)
                    total = e if total is None else total + e
                    at = pl.ds(z * cells + ROWS * k, ROWS)
                    if first:
                        half_way[at, :] = mixed_cells[k] - dry * e
                    else:
                        odd_p[b, at, :] = mixed_cells[k] - dry * e
                sums[0, b, pl.ds(z * ROWS, ROWS), :] = total

            if first:
                sweep(b, even_p, odd_p, cloud)
            else:
                sweep(b, half_way, None, cloud)
            excess = (0.5 * flag) * total_of(0, b)
            mean_p = mean_p + relax_p - DRYING * excess
            condensed = excess if condensed is None else condensed + excess

        ret_out[0, here_rows, :] = jnp.transpose(jnp.concatenate([mean_p, condensed], axis=0), (1, 0))

        def answer(k, _):
            to_dev = jnp.bitwise_xor(dev, k)
            pltpu.make_async_remote_copy(
                rows_of(ret_out, b * per_plane + to_dev, peer_rows), rows_of(ret_in, me, peer_rows), ret_send, ret_recv,
                device_id=(b, to_dev), device_id_type=MESH).start()
            return 0
        lax.fori_loop(jnp.where(far == 0, 1, 0), per_plane, answer, 0)

        @pl.when(far == 0)
        def _():
            pltpu.make_async_copy(rows_of(ret_out, me, peer_rows), rows_of(ret_in, me, peer_rows), ret_recv).start()

        return 0
    lax.fori_loop(0, planes, block, 0)

    def relaxed(mean, aim, m, keep):
        added = None
        for step in range(SUB):
            mean = mixed(mean, m, keep, levels)
            pull = RELAX_RATE * (aim - mean)
            added = pull if added is None else mixed(added, m, keep, levels) + pull
            mean = mean + pull
        return mean, added

    def finish(b, _):
        _, row_c = relaxed(total_of(1, b), coef[b, 6], coef[b, 3] * (1.0 / keep_x), coef[b, 4] * (1.0 / keep_x))
        coef[b, 5] = (coef[b, 5] + (0.5 + 0.5 * row_c)) * (1.0 / DRYING)
        coef[b, 6] = row_c

        def keep_cells(z, mixed_cells):
            for k in range(groups):
                half_way[pl.ds(z * cells + ROWS * k, ROWS), :] = mixed_cells[k]

        def combine(z, mixed_cells):
            add_w, add_c = row(b, 5, z), row(b, 6, z)
            for k in range(groups):
                gap = odd_p[b, pl.ds(z * cells + ROWS * k, ROWS), :]
                w = (gap + 0.5 * mixed_cells[k]) * (1.0 / DRYING) + add_w
                at = pl.ds(z * cells + k, ROWS, stride=groups)
                even_p[b, at, :] = w
                odd_c[b, at, :] = (mixed_cells[k] + add_c) - LATENT_HEAT * w

        sweep(b, even_c, odd_c, keep_cells)
        sweep(b, half_way, None, combine)
        lanes = pl.ds(pl.multiple_of(b * LANES, LANES), LANES)

        def narrow(z, _):
            at = pl.ds(z * cells, cells)
            theta_out[z, :, lanes] = odd_c[b, at, :].astype(theta_out.dtype)
            water_out[z, :, lanes] = even_p[b, at, :].astype(water_out.dtype)
            return 0
        return lax.fori_loop(0, levels, narrow, 0, unroll=29)
    lax.fori_loop(0, planes, finish, 0)
    state_out[...] = state[...]

    pltpu.make_async_copy(start_in, start_in, start_recv).wait()
    source = 2 * iota((columns // 2, columns), 0)
    first_c = (dot(start_in[0], ones_where(source == dest_row), 0, 0)[:zp]
               + dot(start_in[0], ones_where(source + 1 == dest_row), 0, 0)[zp:])
    column_m = 0.1 + 0.15 * jax.nn.sigmoid(state[1, :zp, :])
    column_wet = (state[3, :zp, :] + state[4, :zp, :]) + state[5, :zp, :]
    mean_c, _ = relaxed(first_c, state[2, :zp, :] + LATENT_HEAT * column_wet, column_m, 1.0 - 2.0 * column_m)

    pltpu.make_async_copy(ret_in, ret_in, ret_recv).wait()
    back = dot(ret_in[0], place[...], 0, 0)
    mean_w = (back[:zp] + (0.5 + 0.5 * mean_c)) * (1.0 / DRYING)
    after = {2: mean_c - LATENT_HEAT * mean_w, 3: mean_w, 4: back[zp:]}
    for f, value in after.items():
        old = state[f, :zp, :]
        new = old + STEP_WEIGHT * (value - old)
        state_out[f, :zp, :] = jnp.where(iota((zp, columns), 0) < levels, new, old)

    for ref, sem, count in ((start_out, start_send, peer_rows // 2), (fwd_out, fwd_send, peer_rows), (ret_out, ret_send, peer_rows)):
        gone = ref.at[:, pl.ds(count, (devices - 1) * count), :]
        pltpu.make_async_copy(gone, gone, sem).wait()


def store_kernel(*refs):
    sems = refs[6]
    copies = [pltpu.make_async_copy(refs[i], refs[3 + i], sems.at[i]) for i in range(3)]
    for c in copies:
        c.start()
    for c in copies:
        c.wait()


def on_device(planes, per_plane, column_state, neighbours, crm_slot, cloudy, crm_theta, crm_water):
    fields, lev, columns = column_state.shape
    levels, cells, _ = crm_theta.shape
    zp = -(-levels // ROWS) * ROWS
    elements = columns // 4
    blocks = columns // LANES
    wide, answer = (pltpu.VMEM((n, columns, 2 * zp), F32) for n in (2, 1))
    start = pltpu.VMEM((1, columns // 2, 2 * zp), F32)
    halo = pltpu.VMEM((4 * zp, elements), F32)
    rest = pltpu.VMEM((fields * lev - 3 * zp, elements), F32)
    narrow_block = pltpu.VMEM((blocks, levels, cells, LANES), crm_theta.dtype)
    wide_block = pltpu.VMEM((blocks, levels * cells, LANES), F32)
    dma = pltpu.SemaphoreType.DMA
    hbm, vmem = pl.BlockSpec(memory_space=pl.ANY), pl.BlockSpec(memory_space=pltpu.VMEM)
    inputs = [pltpu.with_memory_space_constraint(a, pltpu.HBM)
              for a in (column_state, neighbours.T, crm_slot, cloudy, crm_theta, crm_water)]
    results = pl.pallas_call(
        functools.partial(step_kernel, (planes, per_plane, levels, cells)),
        out_shape=tuple(jax.ShapeDtypeStruct(a.shape, a.dtype) for a in (column_state, crm_theta, crm_water)),
        in_specs=[hbm] * 6,
        out_specs=(vmem, vmem, vmem),
        scratch_shapes=[
            pltpu.VMEM((4, elements), jnp.int32), pltpu.VMEM((columns,), jnp.int32), pltpu.VMEM((columns,), jnp.int32),
            pltpu.VMEM(column_state.shape, F32), halo, halo, halo, rest, rest, rest, pltpu.VMEM((columns, columns), BF16),
            narrow_block, narrow_block, wide_block, wide_block, wide_block, wide_block,
            pltpu.VMEM((levels * cells, LANES), F32),
            pltpu.VMEM((blocks, 7, zp, LANES), F32), pltpu.VMEM((2, blocks, zp * ROWS, LANES), F32),
            pltpu.VMEM((LANES, LANES), F32), start, start, wide, wide, answer, answer,
            dma((4 + 2 * blocks,)), dma((4,)), dma((4,)), dma, dma, dma, dma((planes,)), dma, dma,
        ],
        compiler_params=pltpu.CompilerParams(collective_id=0, has_side_effects=True, vmem_limit_bytes=36 * 2 ** 20),
        name="physics_step",
    )(*inputs)
    return pl.pallas_call(
        store_kernel,
        out_shape=tuple(jax.ShapeDtypeStruct(a.shape, a.dtype) for a in results),
        in_specs=[vmem] * 3,
        out_specs=(hbm, hbm, hbm),
        scratch_shapes=[dma((3,))],
        compiler_params=pltpu.CompilerParams(vmem_limit_bytes=16 * 2 ** 20),
        name="store",
    )(*results)


def solution(mesh):
    split = ("ga", "dev")
    planes, per_plane = mesh.shape["ga"], mesh.shape["dev"]
    return jax.shard_map(
        functools.partial(on_device, planes, per_plane),
        mesh=mesh,
        in_specs=(P(None, None, split), P(split, None), P(split), P(split), P(None, None, split), P(None, None, split)),
        out_specs=(P(None, None, split), P(None, None, split), P(None, None, split)),
        check_vma=False,
    )
```

```python
import functools

import jax
import jax.numpy as jnp
from jax import lax
from jax.experimental import pallas as pl
from jax.experimental.pallas import tpu as pltpu
from jax.sharding import PartitionSpec as P

SUB = 2
DIFFUSION = 0.15
X_DIFFUSION = 0.2
RELAX_RATE = 0.2
LATENT_HEAT = 0.8
DRYING = 1.0 + 0.5 * LATENT_HEAT
STEP_WEIGHT = 0.5
LANES = 128
ORDER = {4: (2, 1, 3, 0)}
SERVED = {4: (2, 1, 3, 0)}
ROWS = 8
MESH = pl.DeviceIdType.MESH
F32, BF16 = jnp.float32, jnp.bfloat16


def pieces(x):
    high = x.astype(BF16)
    return high, (x - high.astype(F32)).astype(BF16)


def dot(a, b, left=1, right=0):
    dims = (((left,), (right,)), ((), ()))
    one = functools.partial(lax.dot_general, dimension_numbers=dims, preferred_element_type=F32)
    if a.dtype == BF16:
        parts = [one(a, p) for p in pieces(b)]
    else:
        parts = [one(p, b) for p in pieces(a)]
    return parts[1] + parts[0]


def iota(shape, dim):
    return lax.broadcasted_iota(jnp.int32, shape, dim)


def ones_where(mask, value=1.0):
    return jnp.where(mask, value, 0.0).astype(BF16)


def neighbours_of(g):
    east = g[1:] + [pltpu.roll(g[0], ROWS - 1, 0)]
    west = [pltpu.roll(g[-1], 1, 0)] + g[:-1]
    return east, west


def mixed(rows, m, keep, levels):
    up = pltpu.roll(rows, rows.shape[0] - 1, 0)
    down = pltpu.roll(rows, 1, 0)
    z = iota(rows.shape, 0)
    up = jnp.where(z == levels - 1, rows, up)
    down = jnp.where(z == 0, rows, down)
    return keep * rows + m * (up + down)


def step_kernel(sizes, state_hbm, nb_hbm, slot_hbm, cloudy_hbm, theta_hbm, water_hbm,
                state_out, theta_out, water_out,
                nb_ref, slot_ref, cloudy_ref, state, mean, low, high, rest_mean, rest_low, rest_high, place, theta_in, water_in, even_p, odd_p, even_c, odd_c, half_way, coef, sums,
                pack, start_out, start_in, fwd_out, fwd_in, ret_out, ret_in,
                load_sem, halo_send, halo_recv, start_send, start_recv, fwd_send, fwd_recv, ret_send, ret_recv):
    planes, per_plane, levels, cells = sizes
    devices = planes * per_plane
    fields, lev, columns = state.shape
    elements = columns // 4
    peer_rows = columns // devices
    zp = coef.shape[2]
    groups = cells // ROWS
    ga, dev = lax.axis_index("ga"), lax.axis_index("dev")
    me = ga * per_plane + dev
    keep_x = 1.0 - 2.0 * X_DIFFUSION
    side = X_DIFFUSION / keep_x

    load_state = pltpu.make_async_copy(state_hbm, state, load_sem.at[0])
    load_state.start()
    barrier = pltpu.get_barrier_semaphore()

    for far in ORDER[planes]:
        to_ga = lax.rem(ga + far, planes)

        def greet(k, _):
            pl.semaphore_signal(barrier, inc=1, device_id=(to_ga, jnp.bitwise_xor(dev, k)), device_id_type=MESH)
            return 0
        lax.fori_loop(0 if far else 1, per_plane, greet, 0)

    small = [pltpu.make_async_copy(src, dst, load_sem.at[1 + 2 * planes + i]) for i, (src, dst) in enumerate(
        ((nb_hbm, nb_ref), (slot_hbm, slot_ref), (cloudy_hbm, cloudy_ref)))]
    for c in small:
        c.start()
    loads = []
    for b in range(planes):
        for j, (src, dst) in enumerate(((theta_hbm, theta_in), (water_hbm, water_in))):
            loads.append(pltpu.make_async_copy(
                src.at[:, :, pl.ds(b * LANES, LANES)], dst.at[b], load_sem.at[1 + 2 * b + j]))
            loads[-1].start()

    load_state.wait()
    gather = ones_where(iota((columns, elements), 0) // 4 == iota((columns, elements), 1), 0.25)

    def leading():
        total = (state[3, :zp, :] + state[4, :zp, :]) + state[5, :zp, :]
        return jnp.concatenate([state[f, :zp, :] for f in range(3)] + [total], axis=0)

    def trailing():
        return jnp.concatenate([state[f, zp:, :] for f in range(3)] + [state[f] for f in range(3, fields)], axis=0)
    mean[...] = dot(leading(), gather)
    pl.semaphore_wait(barrier, devices - 1)

    def exchange(src, sinks, first):
        copies = []
        for j, (shift, dst) in enumerate(zip((1, devices - 1), sinks)):
            p = lax.rem(me + shift, devices)
            copies.append(pltpu.make_async_remote_copy(
                src, dst, halo_send.at[first + j], halo_recv.at[first + j],
                device_id=(p // per_plane, lax.rem(p, per_plane)), device_id_type=MESH))
            copies[-1].start()
        return copies
    halo = exchange(mean, (low, high), 0)
    rest_mean[...] = dot(trailing(), gather)
    rest_halo = exchange(rest_mean, (rest_low, rest_high), 2)
    for c in small:
        c.wait()

    def rows_of(ref, p, count):
        return ref.at[:, pl.ds(pl.multiple_of(p * count, count), count), :]

    def send_all(src, dst, sent, got, count):
        for far in ORDER[planes]:
            to_ga = lax.rem(ga + (planes - far), planes)

            def send(k, _):
                to_dev = jnp.bitwise_xor(dev, per_plane - 1 - k)
                pltpu.make_async_remote_copy(
                    rows_of(src, to_ga * per_plane + to_dev, count), rows_of(dst, me, count), sent, got(far),
                    device_id=(to_ga, to_dev), device_id_type=MESH).start()
                return 0
            lax.fori_loop(0, per_plane if far else per_plane - 1, send, 0)

    relative = jnp.bitwise_and(nb_ref[...] - me * elements + elements, elements * devices - 1)

    def counts(part):
        total = None
        for k in range(4):
            hit = jnp.where(relative[k:k + 1] - part * elements == iota((elements, elements), 0), 1.0, 0.0)
            total = hit if total is None else total + hit
        return total.astype(BF16)

    slot = slot_ref[...].reshape(1, columns)
    dest_row = slot // columns * peer_rows + lax.rem(slot, peer_rows)
    place[...] = ones_where(iota((columns, columns), 0) == dest_row)
    weights = [counts(part) for part in range(3)]
    own = mean[...]
    laplace = dot(own, weights[1]) - 4.0 * own
    inv = 1.0 / cells
    for c in loads:
        c.wait()

    def widen(i, _):
        b, pair = i // (levels // 2), lax.rem(i, levels // 2)
        for j in range(2):
            z = 2 * pair + j
            warmth, wetness = theta_in[b, z].astype(F32), water_in[b, z].astype(F32)
            gap = (wetness - 0.5 * warmth) - 0.5
            for part, (dst, g) in enumerate(((even_p, gap), (even_c, warmth + LATENT_HEAT * wetness))):
                dst[b, pl.ds(z * cells, cells), :] = g
                sums[part, b, pl.ds(z * ROWS, ROWS), :] = functools.reduce(
                    jnp.add, [g[ROWS * k:ROWS * k + ROWS] for k in range(groups)])
        return 0
    lax.fori_loop(0, planes * levels // 2, widen, 0, unroll=4)

    def slopes(i, _):
        b, pair = i // (levels // 2), lax.rem(i, levels // 2)
        for j in range(2):
            z = 2 * pair + j
            for even, odd in ((even_p, odd_p), (even_c, odd_c)):
                g = [even[b, pl.ds(z * cells + k, ROWS, stride=groups), :] for k in range(groups)]
                east, west = neighbours_of(g)
                for k in range(groups):
                    at = pl.ds(z * cells + ROWS * k, ROWS)
                    even[b, at, :] = g[k] + side * (east[k] + west[k])
                    odd[b, at, :] = east[k] - west[k]
        return 0

    def total_of(part, b):
        rows = [sums[part, b, pl.ds(k, zp, stride=ROWS), :] for k in range(ROWS)]
        return functools.reduce(jnp.add, rows) * inv

    for b in range(planes):
        total = total_of(1, b)
        pack[...] = jnp.transpose(jnp.concatenate([total, total], axis=0), (1, 0))
        evens, odds = pack[pl.ds(0, LANES // 2, stride=2), :], pack[pl.ds(1, LANES // 2, stride=2), :]
        start_out[0, pl.ds(b * (LANES // 2), LANES // 2), :] = jnp.where(iota(evens.shape, 1) < zp, evens, odds)
    halo[0].wait()
    halo[1].wait()
    laplace = laplace + (dot(low[...], weights[0]) + dot(high[...], weights[2]))
    spread = ones_where(iota((elements, columns), 0) == iota((elements, columns), 1) // 4)
    lead = leading() + DIFFUSION * dot(laplace, spread)
    for h in range(2):
        fwd_out[h] = dot(place[...], lead[2 * zp * h:2 * zp * (h + 1)], 1, 1)

    own_fwd = pltpu.make_async_copy(rows_of(fwd_out, me, peer_rows), rows_of(fwd_in, me, peer_rows), fwd_recv.at[0])
    own_fwd.start()

    def ahead(turn):
        out = turn * 0
        for t, far in enumerate(SERVED[planes]):
            out = jnp.where(turn == t, far, out)
        return out

    send_all(fwd_out, fwd_in, fwd_send, lambda far: fwd_recv.at[far], peer_rows)
    state_rest = trailing()
    for f in range(3):
        state[f, :zp, :] = lead[f * zp:(f + 1) * zp]

    lax.fori_loop(0, planes * levels // 2, slopes, 0, unroll=4)
    own_start = pltpu.make_async_copy(
        rows_of(start_out, me, peer_rows // 2), rows_of(start_in, me, peer_rows // 2), start_recv)
    own_start.start()
    send_all(start_out, start_in, start_send, lambda far: start_recv, peer_rows // 2)


    rest_halo[0].wait()
    rest_halo[1].wait()
    own = rest_mean[...]
    laplace = (dot(own, weights[1]) - 4.0 * own) + (dot(rest_low[...], weights[0]) + dot(rest_high[...], weights[2]))
    state_rest = state_rest + DIFFUSION * dot(laplace, spread)
    tops = lev - zp
    for f in range(3):
        state[f, zp:, :] = state_rest[f * tops:(f + 1) * tops]
        state[3 + f] = state_rest[3 * tops + f * lev:3 * tops + (f + 1) * lev]

    def row(b, i, z):
        return jnp.broadcast_to(coef[b, i, pl.ds(z, 1), :], (ROWS, LANES))

    def sweep(b, even, odd, store):
        def strip(ref, z, k):
            at = pl.ds(z * cells + ROWS * k, ROWS)
            return ref[at, :] if ref is half_way else ref[b, at, :]

        def advected(z):
            g = [strip(even, z, k) for k in range(groups)]
            if odd is not None:
                rate = row(b, 0, z)
                return [g[k] - rate * strip(odd, z, k) for k in range(groups)]
            east_c, west_c = row(b, 1, z), row(b, 2, z)
            east, west = neighbours_of(g)
            return [g[k] + (east_c * east[k] + west_c * west[k]) for k in range(groups)]

        def mix(z, below, here, above):
            mz, kz = row(b, 3, z), row(b, 4, z)
            store(z, [kz * here[k] + mz * (above[k] + below[k]) for k in range(groups)])

        def body(z, carry):
            below, here = carry
            above = advected(z + 1)
            mix(z, below, here, above)
            return here, above

        edge = advected(0)
        below, here = lax.fori_loop(0, levels - 1, body, (edge, edge), unroll=19)
        mix(levels - 1, below, here, here)

    def block(turn, _):
        far = ahead(turn)
        b = lax.rem(ga + far, planes)
        here_rows = pl.ds(pl.multiple_of(b * LANES, LANES), LANES)
        arrived = fwd_in.at[:, here_rows, :]
        pltpu.make_async_copy(arrived, arrived, fwd_recv.at[far]).wait()
        wind = jnp.transpose(fwd_in[0, here_rows, :], (1, 0))
        heat_wet = jnp.transpose(fwd_in[1, here_rows, :], (1, 0))
        heat, wet = heat_wet[:zp], heat_wet[zp:]
        slope = (0.15 / keep_x) * jnp.tanh(wind[:zp])
        m = 0.1 + 0.15 * jax.nn.sigmoid(wind[zp:])
        keep = 1.0 - 2.0 * m
        for i, rows in enumerate((slope, side - slope, side + slope, keep_x * m, keep_x * keep)):
            coef[b, i] = rows
        flag = cloudy_ref[here_rows].astype(F32).reshape(1, LANES)
        dry = jnp.broadcast_to((0.5 * DRYING) * flag, (ROWS, LANES))
        mean_p = total_of(0, b)
        aim_p = (wet - 0.5 * heat) - 0.5
        coef[b, 6] = heat + LATENT_HEAT * wet
        row_p = condensed = None

        for step in range(SUB):
            first = step == 0
            mean_p = mixed(mean_p, m, keep, levels)
            relax_p = RELAX_RATE * (aim_p - mean_p)
            row_p = relax_p if first else mixed(row_p, m, keep, levels) + relax_p
            coef[b, 5] = row_p

            def cloud(z, mixed_cells):
                offset = row(b, 5, z)
                total = None
                for k in range(groups):
                    e = jnp.maximum(mixed_cells[k] + offset, 0.0)
                    total = e if total is None else total + e
                    at = pl.ds(z * cells + ROWS * k, ROWS)
                    if first:
                        half_way[at, :] = mixed_cells[k] - dry * e
                    else:
                        odd_p[b, at, :] = mixed_cells[k] - dry * e
                sums[0, b, pl.ds(z * ROWS, ROWS), :] = total

            if first:
                sweep(b, even_p, odd_p, cloud)
            else:
                sweep(b, half_way, None, cloud)
            excess = (0.5 * flag) * total_of(0, b)
            mean_p = mean_p + relax_p - DRYING * excess
            condensed = excess if condensed is None else condensed + excess

        ret_out[0, here_rows, :] = jnp.transpose(jnp.concatenate([mean_p, condensed], axis=0), (1, 0))

        def answer(k, _):
            to_dev = jnp.bitwise_xor(dev, per_plane - 1 - k)
            pltpu.make_async_remote_copy(
                rows_of(ret_out, b * per_plane + to_dev, peer_rows), rows_of(ret_in, me, peer_rows), ret_send, ret_recv,
                device_id=(b, to_dev), device_id_type=MESH).start()
            return 0
        lax.fori_loop(0, jnp.where(far == 0, per_plane - 1, per_plane), answer, 0)

        @pl.when(far == 0)
        def _():
            pltpu.make_async_copy(rows_of(ret_out, me, peer_rows), rows_of(ret_in, me, peer_rows), ret_recv).start()

        return 0
    lax.fori_loop(0, planes, block, 0)

    def relaxed(mean, aim, m, keep):
        added = None
        for step in range(SUB):
            mean = mixed(mean, m, keep, levels)
            pull = RELAX_RATE * (aim - mean)
            added = pull if added is None else mixed(added, m, keep, levels) + pull
            mean = mean + pull
        return mean, added

    def finish(b, _):
        _, row_c = relaxed(total_of(1, b), coef[b, 6], coef[b, 3] * (1.0 / keep_x), coef[b, 4] * (1.0 / keep_x))
        coef[b, 5] = (coef[b, 5] + (0.5 + 0.5 * row_c)) * (1.0 / DRYING)
        coef[b, 6] = row_c

        def keep_cells(z, mixed_cells):
            for k in range(groups):
                half_way[pl.ds(z * cells + ROWS * k, ROWS), :] = mixed_cells[k]

        def combine(z, mixed_cells):
            add_w, add_c = row(b, 5, z), row(b, 6, z)
            for k in range(groups):
                gap = odd_p[b, pl.ds(z * cells + ROWS * k, ROWS), :]
                w = (gap + 0.5 * mixed_cells[k]) * (1.0 / DRYING) + add_w
                at = pl.ds(z * cells + k, ROWS, stride=groups)
                even_p[b, at, :] = w
                odd_c[b, at, :] = (mixed_cells[k] + add_c) - LATENT_HEAT * w

        sweep(b, even_c, odd_c, keep_cells)
        sweep(b, half_way, None, combine)
        lanes = pl.ds(pl.multiple_of(b * LANES, LANES), LANES)

        def narrow(z, _):
            at = pl.ds(z * cells, cells)
            theta_out[z, :, lanes] = odd_c[b, at, :].astype(theta_out.dtype)
            water_out[z, :, lanes] = even_p[b, at, :].astype(water_out.dtype)
            return 0
        return lax.fori_loop(0, levels, narrow, 0, unroll=29)
    lax.fori_loop(0, planes, finish, 0)
    state_out[...] = state[...]

    pltpu.make_async_copy(start_in, start_in, start_recv).wait()
    source = 2 * iota((columns // 2, columns), 0)
    first_c = (dot(start_in[0], ones_where(source == dest_row), 0, 0)[:zp]
               + dot(start_in[0], ones_where(source + 1 == dest_row), 0, 0)[zp:])
    column_m = 0.1 + 0.15 * jax.nn.sigmoid(state[1, :zp, :])
    column_wet = (state[3, :zp, :] + state[4, :zp, :]) + state[5, :zp, :]
    mean_c, _ = relaxed(first_c, state[2, :zp, :] + LATENT_HEAT * column_wet, column_m, 1.0 - 2.0 * column_m)

    pltpu.make_async_copy(ret_in, ret_in, ret_recv).wait()
    back = dot(ret_in[0], place[...], 0, 0)
    mean_w = (back[:zp] + (0.5 + 0.5 * mean_c)) * (1.0 / DRYING)
    after = {2: mean_c - LATENT_HEAT * mean_w, 3: mean_w, 4: back[zp:]}
    for f, value in after.items():
        old = state[f, :zp, :]
        new = old + STEP_WEIGHT * (value - old)
        state_out[f, :zp, :] = jnp.where(iota((zp, columns), 0) < levels, new, old)

    for ref, sem, count in ((start_out, start_send, peer_rows // 2), (fwd_out, fwd_send, peer_rows), (ret_out, ret_send, peer_rows)):
        gone = ref.at[:, pl.ds(count, (devices - 1) * count), :]
        pltpu.make_async_copy(gone, gone, sem).wait()


def store_kernel(*refs):
    sems = refs[6]
    copies = [pltpu.make_async_copy(refs[i], refs[3 + i], sems.at[i]) for i in range(3)]
    for c in copies:
        c.start()
    for c in copies:
        c.wait()


def on_device(planes, per_plane, column_state, neighbours, crm_slot, cloudy, crm_theta, crm_water):
    fields, lev, columns = column_state.shape
    levels, cells, _ = crm_theta.shape
    zp = -(-levels // ROWS) * ROWS
    elements = columns // 4
    blocks = columns // LANES
    wide, answer = (pltpu.VMEM((n, columns, 2 * zp), F32) for n in (2, 1))
    start = pltpu.VMEM((1, columns // 2, 2 * zp), F32)
    halo = pltpu.VMEM((4 * zp, elements), F32)
    rest = pltpu.VMEM((fields * lev - 3 * zp, elements), F32)
    narrow_block = pltpu.VMEM((blocks, levels, cells, LANES), crm_theta.dtype)
    wide_block = pltpu.VMEM((blocks, levels * cells, LANES), F32)
    dma = pltpu.SemaphoreType.DMA
    hbm, vmem = pl.BlockSpec(memory_space=pl.ANY), pl.BlockSpec(memory_space=pltpu.VMEM)
    inputs = [pltpu.with_memory_space_constraint(a, pltpu.HBM)
              for a in (column_state, neighbours.T, crm_slot, cloudy, crm_theta, crm_water)]
    results = pl.pallas_call(
        functools.partial(step_kernel, (planes, per_plane, levels, cells)),
        out_shape=tuple(jax.ShapeDtypeStruct(a.shape, a.dtype) for a in (column_state, crm_theta, crm_water)),
        in_specs=[hbm] * 6,
        out_specs=(vmem, vmem, vmem),
        scratch_shapes=[
            pltpu.VMEM((4, elements), jnp.int32), pltpu.VMEM((columns,), jnp.int32), pltpu.VMEM((columns,), jnp.int32),
            pltpu.VMEM(column_state.shape, F32), halo, halo, halo, rest, rest, rest, pltpu.VMEM((columns, columns), BF16),
            narrow_block, narrow_block, wide_block, wide_block, wide_block, wide_block,
            pltpu.VMEM((levels * cells, LANES), F32),
            pltpu.VMEM((blocks, 7, zp, LANES), F32), pltpu.VMEM((2, blocks, zp * ROWS, LANES), F32),
            pltpu.VMEM((LANES, LANES), F32), start, start, wide, wide, answer, answer,
            dma((4 + 2 * blocks,)), dma((4,)), dma((4,)), dma, dma, dma, dma((planes,)), dma, dma,
        ],
        compiler_params=pltpu.CompilerParams(collective_id=0, has_side_effects=True, vmem_limit_bytes=36 * 2 ** 20),
        name="physics_step",
    )(*inputs)
    return pl.pallas_call(
        store_kernel,
        out_shape=tuple(jax.ShapeDtypeStruct(a.shape, a.dtype) for a in results),
        in_specs=[vmem] * 3,
        out_specs=(hbm, hbm, hbm),
        scratch_shapes=[dma((3,))],
        compiler_params=pltpu.CompilerParams(vmem_limit_bytes=16 * 2 ** 20),
        name="store",
    )(*results)


def solution(mesh):
    split = ("ga", "dev")
    planes, per_plane = mesh.shape["ga"], mesh.shape["dev"]
    return jax.shard_map(
        functools.partial(on_device, planes, per_plane),
        mesh=mesh,
        in_specs=(P(None, None, split), P(split, None), P(split), P(split), P(None, None, split), P(None, None, split)),
        out_specs=(P(None, None, split), P(None, None, split), P(None, None, split)),
        check_vma=False,
    )
```
